32 devices in a mesh: seq: 8 (over y, x, core), head: 4 (over z).
Axes of the slice: x: 2, y: 2, z: 4, core: 2. Of those that a mesh axis runs over, the one named last changes fastest.
Arguments:
- queries: bfloat16 [8192, 8192], P(('seq', 'head')), may hold values from -64 to 64
- key_rows: bfloat16 [8192, 1024], P(('seq', 'head')), may hold values from -6 to 6
- value_projection_rows: bfloat16 [8192, 1024], P(('seq', 'head')), may hold values from -6 to 6
- upstream: bfloat16 [8192, 8192], P(('seq', 'head')), may hold values from -6 to 6
- ancestors: int32 [128, 2], P('seq'), may hold values from -1 to 126, as said below
Outputs:
- attended: bfloat16 [8192, 8192], P(('seq', 'head'))
- query_grad: bfloat16 [8192, 8192], P(('seq', 'head'))
- key_grad: bfloat16 [8192, 1024], P(('seq', 'head'))
- value_grad: bfloat16 [8192, 1024], P(('seq', 'head'))
The draws below stay inside these ranges and needn't reach their ends.
Inputs may be any that keep to these rules, and one draw needn't show every extreme that they name: `ancestors`: each entry of row b is -1 (no ancestor) or a block index from max(1, b - 32) to b - 1; where that range is not empty the first entry is b - 1, and where b is a multiple of 16 the last entry is the lowest index of that range. Entries of a row may repeat.
All inputs are finite; a program needn't handle non-finite values.
Results may differ from the reference program's by a relative error of at most 0.012.
The reference program's roundings to bfloat16 on the way (of `probs` and `dscore`) count: a program that leaves them out, or rounds other values in their place, can miss the bound.
Values may be sent and summed in bfloat16 or wider, within the bound.
A program may use at most 192 MiB of HBM per device.

```python
import jax
import jax.numpy as jnp
from jax import lax

QUERY_HEAD_COUNT = 64
KEY_VALUE_HEADS = 8
HEAD_SIZE = 128
MASK_BLOCK_SIZE = 64
ROOT = 64
ANC = 2
PACKED_TOKENS = 8192
ROW_MASK_BLOCKS = 128
BPS = 16


def base_keys(key):
    source = jax.random.fold_in(key, 101)
    array_shape = (PACKED_TOKENS, KEY_VALUE_HEADS * HEAD_SIZE)
    value_matrix = jnp.clip(jax.random.normal(source, array_shape, jnp.float32), -6.0, 6.0)
    return value_matrix


def draw_key_rows(key, part):
    return base_keys(key).astype(jnp.bfloat16)


def draw_queries(key, part):
    source = jax.random.fold_in(key, 202)
    array_shape = (PACKED_TOKENS, QUERY_HEAD_COUNT * HEAD_SIZE)
    value_matrix = jnp.clip(jax.random.normal(source, array_shape, jnp.float32), -6.0, 6.0)
    return value_matrix.astype(jnp.bfloat16)


def draw_ancestors(key, part):
    block = jnp.arange(ROW_MASK_BLOCKS, dtype=jnp.int32)[:, None]
    lowest = jnp.maximum(ROOT // MASK_BLOCK_SIZE, block - 2 * BPS)
    highest = block - 1
    span = highest - lowest + 1
    raw = jax.random.randint(jax.random.fold_in(key, 303), (ROW_MASK_BLOCKS, ANC), 0, 1048576, jnp.int32)
    picked = lowest + raw % jnp.maximum(span, 1)
    shard_start = block % BPS == 0
    drawn_count = jax.random.randint(jax.random.fold_in(key, 304), (ROW_MASK_BLOCKS, 1), 1, ANC + 1, jnp.int32)
    count = jnp.where(shard_start, ANC, drawn_count)
    column = jnp.arange(ANC, dtype=jnp.int32)[None, :]
    entry = jnp.where(shard_start & (column == ANC - 1), lowest, picked)
    entry = jnp.where(column == 0, highest, entry)
    return jnp.where((column < count) & (span > 0), entry, -1).astype(jnp.int32)


def block_scale(key, extent, pieces, least, top_value):
    loudness = 1.0
    for position, blocks in pieces:
        heights = jax.random.uniform(jax.random.fold_in(jax.random.fold_in(key, 6), position), (blocks,), jnp.float32, least / len(pieces), top_value / len(pieces))
        loudness = loudness * jnp.repeat(jnp.exp(heights), extent[position] // blocks).reshape((-1,) + (1,) * (len(extent) - 1 - position))
    return loudness


def scatter_about(own_key, extent, deviation, limit, cuts=(), kind=jnp.bfloat16):
    factor_of = block_scale(own_key, extent, cuts, -0.22, 0.18) if cuts else 1.0
    values = jax.random.normal(own_key, extent, jnp.float32) * deviation * factor_of
    return jnp.minimum(jnp.maximum(values, -limit), limit).astype(kind)


def setup_inputs(seed: int = 0) -> dict:
    streams_of = jax.random.split(jax.random.key(seed), 6)
    return {
        "queries": draw_queries(jax.random.fold_in(streams_of[5], 71), 0),
        "key_rows": draw_key_rows(jax.random.fold_in(streams_of[5], 71), 0),
        "value_projection_rows": scatter_about(streams_of[2], (PACKED_TOKENS, KEY_VALUE_HEADS * HEAD_SIZE), 1.0, 6.0, ((0, 32),)),
        "upstream": scatter_about(streams_of[3], (PACKED_TOKENS, QUERY_HEAD_COUNT * HEAD_SIZE), 1.0, 6.0, ((0, 32),)),
        "ancestors": draw_ancestors(jax.random.fold_in(streams_of[5], 71), 0),
    }


NEGATIVE = -1.0e30


def distinct_entries(ancestor_row):
    order = jnp.arange(ANC, dtype=jnp.int32)
    before = order[None, :] < order[:, None]
    repeated = jnp.any((ancestor_row[:, None] == ancestor_row[None, :]) & before, axis=1)
    return (ancestor_row >= 0) & jnp.logical_not(repeated)


def reference(queries, key_rows, value_projection_rows, upstream, ancestors):
    query_groups = QUERY_HEAD_COUNT // KEY_VALUE_HEADS
    scale = HEAD_SIZE ** -0.5
    head_width = KEY_VALUE_HEADS * HEAD_SIZE
    blocked_keys = key_rows.reshape(ROW_MASK_BLOCKS, MASK_BLOCK_SIZE, head_width)
    blocked_values = value_projection_rows.reshape(ROW_MASK_BLOCKS, MASK_BLOCK_SIZE, head_width)
    tree_root_key = key_rows[:ROOT]
    tree_root_value = value_projection_rows[:ROOT]
    query_blocks = queries.reshape(ROW_MASK_BLOCKS, MASK_BLOCK_SIZE, QUERY_HEAD_COUNT * HEAD_SIZE)
    upstream_blocks = upstream.reshape(ROW_MASK_BLOCKS, MASK_BLOCK_SIZE, QUERY_HEAD_COUNT * HEAD_SIZE)
    inner = jnp.arange(MASK_BLOCK_SIZE, dtype=jnp.int32)

    def step(carry, inputs):
        key_acc, value_acc = carry
        block_index, blocked_query, blocked_upstream, ancestor_row = inputs
        valid = distinct_entries(ancestor_row)
        picked = jnp.maximum(ancestor_row, 0).astype(jnp.int32)
        ancestor_key = blocked_keys[picked].reshape(ANC * MASK_BLOCK_SIZE, head_width)
        ancestor_value = blocked_values[picked].reshape(ANC * MASK_BLOCK_SIZE, head_width)
        key_matrix = jnp.concatenate([tree_root_key, blocked_keys[block_index], ancestor_key], 0).astype(jnp.float32).reshape(-1, KEY_VALUE_HEADS, HEAD_SIZE)
        value_matrix = jnp.concatenate([tree_root_value, blocked_values[block_index], ancestor_value], 0).astype(jnp.float32).reshape(-1, KEY_VALUE_HEADS, HEAD_SIZE)
        query_pos = (block_index * MASK_BLOCK_SIZE + inner).astype(jnp.int32)
        root_pos = jnp.arange(ROOT, dtype=jnp.int32)
        anc_rows = (picked[:, None] * MASK_BLOCK_SIZE + inner[None, :]).reshape(-1).astype(jnp.int32)
        root_mask = root_pos[None, :] <= query_pos[:, None]
        own_mask = (query_pos[None, :] <= query_pos[:, None]) & (query_pos[None, :] >= ROOT)
        anc_mask = jnp.broadcast_to(jnp.repeat(valid, MASK_BLOCK_SIZE)[None, :], (MASK_BLOCK_SIZE, ANC * MASK_BLOCK_SIZE))
        mask = jnp.concatenate([root_mask, own_mask, anc_mask], 1)
        heads_of_query = blocked_query.astype(jnp.float32).reshape(MASK_BLOCK_SIZE, KEY_VALUE_HEADS, query_groups, HEAD_SIZE)
        scores = jnp.einsum("qkgd,skd->kgqs", heads_of_query, key_matrix) * scale
        masked = jnp.where(mask, scores, NEGATIVE)
        row_top = jnp.max(masked, axis=-1, keepdims=True)
        row_total = jnp.sum(jnp.where(mask, jnp.exp(masked - row_top), 0.0), axis=-1, keepdims=True)
        lse = row_top + jnp.log(row_total)
        probs = lax.optimization_barrier(jnp.where(mask, jnp.exp(masked - lse), 0.0).astype(jnp.bfloat16)).astype(jnp.float32)
        attended = lax.optimization_barrier(jnp.einsum("kgqs,skd->qkgd", probs, value_matrix).astype(jnp.bfloat16))
        heads_of_upstream = blocked_upstream.astype(jnp.float32).reshape(MASK_BLOCK_SIZE, KEY_VALUE_HEADS, query_groups, HEAD_SIZE)
        delta = jnp.sum(heads_of_upstream * attended.astype(jnp.float32), axis=-1).transpose(1, 2, 0)[..., None]
        dprob = jnp.einsum("qkgd,skd->kgqs", heads_of_upstream, value_matrix)
        dscore = lax.optimization_barrier((probs * (dprob - delta)).astype(jnp.bfloat16)).astype(jnp.float32)
        query_grad = (scale * jnp.einsum("kgqs,skd->qkgd", dscore, key_matrix)).astype(jnp.bfloat16)
        key_grad = (scale * jnp.einsum("kgqs,qkgd->skd", dscore, heads_of_query)).reshape(-1, head_width)
        value_grad = jnp.einsum("kgqs,qkgd->skd", probs, heads_of_upstream).reshape(-1, head_width)
        rows = jnp.concatenate([root_pos, query_pos, anc_rows], 0).astype(jnp.int32)
        key_acc = key_acc.at[rows].add(key_grad)
        value_acc = value_acc.at[rows].add(value_grad)
        return (key_acc, value_acc), (attended.reshape(MASK_BLOCK_SIZE, QUERY_HEAD_COUNT * HEAD_SIZE), query_grad.reshape(MASK_BLOCK_SIZE, QUERY_HEAD_COUNT * HEAD_SIZE))

    start_carry = (jnp.zeros((PACKED_TOKENS, head_width), jnp.float32), jnp.zeros((PACKED_TOKENS, head_width), jnp.float32))
    carry, stacked = lax.scan(step, start_carry, (jnp.arange(ROW_MASK_BLOCKS, dtype=jnp.int32), query_blocks, upstream_blocks, ancestors))
    key_acc, value_acc = carry
    attended = stacked[0].reshape(PACKED_TOKENS, QUERY_HEAD_COUNT * HEAD_SIZE)
    query_grad = stacked[1].reshape(PACKED_TOKENS, QUERY_HEAD_COUNT * HEAD_SIZE)
    return (attended, query_grad, key_acc.astype(jnp.bfloat16), value_acc.astype(jnp.bfloat16))
```

```python
import functools
import math

import jax
import jax.numpy as jnp
from jax import lax
from jax.experimental import pallas as pl
from jax.experimental.pallas import tpu as pltpu
from jax.sharding import PartitionSpec as P

HEAD_SIZE = 128
BLOCK = 64
NEGATIVE = -1e30
CHUNKS = 2


def shifted(x, axis, by):
    length = lax.axis_size(axis)
    pairs = [(i, i + by) for i in range(length) if 0 <= i + by < length]
    return lax.ppermute(x, axis, pairs)


def spread_from_first(x, axis):
    length = lax.axis_size(axis)
    step = 1
    while step < length:
        pairs = [(i, i + step) for i in range(step) if i + step < length]
        x = x + lax.ppermute(x, axis, pairs)
        step *= 2
    return x


def sum_to_first(x, axis):
    length = lax.axis_size(axis)
    step = 1
    while step < length:
        step *= 2
    while step > 1:
        step //= 2
        pairs = [(i + step, i) for i in range(step) if i + step < length]
        x = x + lax.ppermute(x, axis, pairs)
    return x


def attention_kernel(
    info, q_ref, up_ref, own_ref, before_ref, edge_ref, root_ref, rand_ref, *rest, groups, aliased
):
    if aliased:
        rest = rest[2:]
    att_ref, dq_ref, g_own, g_prev, g_rand, g_root = rest
    j = pl.program_id(1)
    scale = HEAD_SIZE ** (-0.5)
    first = info[0] + j == 0
    rows = groups * BLOCK
    q = jnp.concatenate(
        [q_ref[:, r * HEAD_SIZE : (r + 1) * HEAD_SIZE] for r in range(groups)], axis=0
    )
    up = jnp.concatenate(
        [up_ref[:, r * HEAD_SIZE : (r + 1) * HEAD_SIZE] for r in range(groups)], axis=0
    )
    prev = jnp.where(j == 0, edge_ref[0], before_ref[0])
    keys = jnp.concatenate([root_ref[0, 0], own_ref[0, 0], prev[0], rand_ref[0, 0]], axis=0)
    values = jnp.concatenate([root_ref[0, 1], own_ref[0, 1], prev[1], rand_ref[0, 1]], axis=0)
    up_t = up.T
    scores = lax.dot_general(
        keys, q, (((1,), (1,)), ((), ())), preferred_element_type=jnp.float32
    ) * (scale * math.log2(math.e))
    key_at = lax.broadcasted_iota(jnp.int32, (BLOCK, rows), 0)
    query_at = lax.broadcasted_iota(jnp.int32, (BLOCK, rows), 1) & (BLOCK - 1)
    causal = key_at <= query_at
    never = jnp.float32(NEGATIVE)
    zero = jnp.float32(0.0)
    root_off = jnp.where(causal, zero, jnp.where(first, never, zero))
    own_off = jnp.where(causal, jnp.where(first, never, zero), never)
    prev_off = jnp.where(info[1 + 2 * j] > 0, zero, never)
    rand_off = jnp.where(info[2 + 2 * j] > 0, zero, never)
    scores = jnp.concatenate(
        [
            scores[:BLOCK] + root_off,
            scores[BLOCK : 2 * BLOCK] + own_off,
            scores[2 * BLOCK : 3 * BLOCK] + prev_off,
            scores[3 * BLOCK :] + rand_off,
        ],
        axis=0,
    )
    top = jnp.max(scores, axis=0, keepdims=True)
    weights = jnp.exp2(scores - top)
    total = jnp.sum(weights, axis=0, keepdims=True)
    probs = (weights * (1.0 / total)).astype(jnp.bfloat16)
    att_t = lax.dot_general(
        values, probs, (((0,), (0,)), ((), ())), preferred_element_type=jnp.float32
    ).astype(jnp.bfloat16)
    delta = jnp.sum(
        att_t.astype(jnp.float32) * up_t.astype(jnp.float32), axis=0, keepdims=True
    )
    dprob = lax.dot_general(
        values, up_t, (((1,), (0,)), ((), ())), preferred_element_type=jnp.float32
    )
    dscore = (probs.astype(jnp.float32) * (dprob - delta)).astype(jnp.bfloat16)
    dq_t = lax.dot_general(
        keys, dscore, (((0,), (0,)), ((), ())), preferred_element_type=jnp.float32
    )
    dq = (dq_t * scale).astype(jnp.bfloat16).T
    att = att_t.T
    for r in range(groups):
        att_ref[:, r * HEAD_SIZE : (r + 1) * HEAD_SIZE] = att[r * BLOCK : (r + 1) * BLOCK]
        dq_ref[:, r * HEAD_SIZE : (r + 1) * HEAD_SIZE] = dq[r * BLOCK : (r + 1) * BLOCK]
    dkey = scale * jnp.dot(dscore, q, preferred_element_type=jnp.float32)
    dvalue = jnp.dot(probs, up, preferred_element_type=jnp.float32)
    g_own[0, 0] = dkey[BLOCK : 2 * BLOCK]
    g_own[0, 1] = dvalue[BLOCK : 2 * BLOCK]
    g_prev[0, 0] = dkey[2 * BLOCK : 3 * BLOCK]
    g_prev[0, 1] = dvalue[2 * BLOCK : 3 * BLOCK]
    g_rand[0, 0] = dkey[3 * BLOCK :].astype(jnp.bfloat16)
    g_rand[0, 1] = dvalue[3 * BLOCK :].astype(jnp.bfloat16)

    @pl.when(j == 0)
    def _():
        g_root[...] = jnp.zeros_like(g_root)

    g_root[0] += dkey[:BLOCK]
    g_root[1] += dvalue[:BLOCK]


def attention(info, queries, upstream, own, edge, root, rand, earlier, chunk, chunk_heads):
    blocks = own.shape[0]
    width = chunk_heads * HEAD_SIZE
    groups = queries.shape[1] // own.shape[3]
    wide = groups * HEAD_SIZE
    start = chunk * chunk_heads
    token_spec = pl.BlockSpec((BLOCK, wide), lambda g, j, _: (j, start + g))
    set_shape = (1, 2, BLOCK, HEAD_SIZE)
    in_specs = [
        token_spec,
        token_spec,
        pl.BlockSpec(set_shape, lambda g, j, _: (j, 0, 0, start + g)),
        pl.BlockSpec(set_shape, lambda g, j, _: (jnp.maximum(j - 1, 0), 0, 0, start + g)),
        pl.BlockSpec(set_shape, lambda g, j, _: (0, 0, 0, start + g)),
        pl.BlockSpec(set_shape, lambda g, j, _: (0, 0, 0, start + g)),
        pl.BlockSpec(set_shape, lambda g, j, _: (j, 0, 0, g)),
    ]
    operands = [queries, upstream, own, own, edge, root, rand]
    aliases = {}
    if earlier is not None:
        in_specs += [pl.BlockSpec(memory_space=pl.ANY)] * 2
        operands += list(earlier)
        aliases = {8: 0, 9: 1}
    by_block = pl.BlockSpec(set_shape, lambda g, j, _: (j, 0, 0, g))
    set_array = (blocks, 2, BLOCK, width)
    elements = blocks * chunk_heads * groups * BLOCK * 4 * BLOCK
    return pl.pallas_call(
        functools.partial(attention_kernel, groups=groups, aliased=earlier is not None),
        grid_spec=pltpu.PrefetchScalarGridSpec(
            num_scalar_prefetch=1,
            grid=(chunk_heads, blocks),
            in_specs=in_specs,
            out_specs=[
                token_spec,
                token_spec,
                by_block,
                by_block,
                by_block,
                pl.BlockSpec((2, BLOCK, HEAD_SIZE), lambda g, j, _: (0, 0, g)),
            ],
        ),
        out_shape=[
            jax.ShapeDtypeStruct(queries.shape, jnp.bfloat16),
            jax.ShapeDtypeStruct(queries.shape, jnp.bfloat16),
            jax.ShapeDtypeStruct(set_array, jnp.float32),
            jax.ShapeDtypeStruct(set_array, jnp.float32),
            jax.ShapeDtypeStruct(set_array, jnp.bfloat16),
            jax.ShapeDtypeStruct((2, BLOCK, width), jnp.float32),
        ],
        input_output_aliases=aliases,
        cost_estimate=pl.CostEstimate(
            flops=12 * elements * HEAD_SIZE,
            transcendentals=elements,
            bytes_accessed=blocks * chunk_heads * wide * BLOCK * 8,
        ),
        compiler_params=pltpu.CompilerParams(vmem_limit_bytes=40 * 1024 * 1024),
        name="attention",
    )(info, *operands)


def place_kernel(index, own_ref, near_ref, far_ref, out_ref, total):
    slots = own_ref.shape[0]
    count = out_ref.shape[0]
    total[...] = jnp.zeros_like(total)
    for part, ref in enumerate((own_ref, near_ref, far_ref)):
        for n in range(slots):
            at = index[part * slots + n]
            inside = jnp.logical_and(at >= 0, at < count)

            @pl.when(inside)
            def _(at=at, ref=ref, n=n):
                total[jnp.clip(at, 0, count - 1)] += ref[n].astype(jnp.float32)

    out_ref[...] = total[...].astype(jnp.bfloat16)


def place(index, own, near, far, count):
    slots, _, _, width = own.shape
    tile = 128
    spec = pl.BlockSpec((slots, 2, BLOCK, tile), lambda g, _: (0, 0, 0, g))
    return pl.pallas_call(
        place_kernel,
        grid_spec=pltpu.PrefetchScalarGridSpec(
            num_scalar_prefetch=1,
            grid=(width // tile,),
            in_specs=[spec] * 3,
            out_specs=pl.BlockSpec((count, 2, BLOCK, tile), lambda g, _: (0, 0, 0, g)),
            scratch_shapes=[pltpu.VMEM((count, 2, BLOCK, tile), jnp.float32)],
        ),
        out_shape=jax.ShapeDtypeStruct((count, 2, BLOCK, width), jnp.bfloat16),
        cost_estimate=pl.CostEstimate(
            flops=count * 2 * BLOCK * width,
            transcendentals=0,
            bytes_accessed=(3 * slots + count) * 2 * BLOCK * width * 2,
        ),
        name="place",
    )(index, own, near, far)


def local(queries, key_rows, value_rows, upstream, ancestors):
    tokens, width = key_rows.shape
    blocks = tokens // BLOCK
    shard_blocks = ancestors.shape[0]
    both = ("seq", "head")
    shard, part = lax.axis_index("seq"), lax.axis_index("head")
    origin = shard * shard_blocks
    mine = lax.dynamic_slice_in_dim(ancestors, part * blocks, blocks, 0)
    first_entry, last_entry = mine[:, 0], mine[:, 1]
    use_prev = first_entry >= 0
    use_rand = (last_entry >= 0) & (last_entry != first_entry)
    info = jnp.concatenate(
        [
            (origin + part * blocks)[None].astype(jnp.int32),
            jnp.stack([use_prev, use_rand], 1).reshape(-1).astype(jnp.int32),
        ]
    )
    wanted_near = shifted(last_entry, "seq", -1) - origin
    wanted_far = shifted(last_entry, "seq", -2) - origin
    wanted_own = last_entry - origin
    length = lax.axis_size("seq")
    wanted_near = jnp.where(shard + 1 < length, wanted_near, -1)
    wanted_far = jnp.where(shard + 2 < length, wanted_far, -1)
    wanted = jnp.concatenate([wanted_own, wanted_near, wanted_far]).astype(jnp.int32)

    own = jnp.stack(
        [key_rows.reshape(blocks, BLOCK, width), value_rows.reshape(blocks, BLOCK, width)], 1
    )
    chunk_heads = width // HEAD_SIZE // CHUNKS
    chunk_width = chunk_heads * HEAD_SIZE
    is_first = (shard == 0) & (part == 0)
    edge = shifted(own[-1:], both, 1)
    root = jnp.where(is_first, own[:1], jnp.zeros_like(own[:1]))
    root = spread_from_first(spread_from_first(root, "head"), "seq")

    def at(x, index):
        return jnp.take(x, jnp.clip(index, 0, shard_blocks - 1), axis=0)

    rands = []
    back = shard - last_entry // shard_blocks
    for c in range(CHUNKS):
        piece = own[..., c * chunk_width : (c + 1) * chunk_width]
        whole = lax.all_gather(piece, "head", axis=0, tiled=True)
        near = shifted(at(whole, wanted_near), "seq", 1)
        far = shifted(at(whole, wanted_far), "seq", 2)
        pick = back[:, None, None, None]
        rands.append(
            jnp.where(pick == 0, at(whole, wanted_own), jnp.where(pick == 1, near, far))
        )
    outs = None
    key_grads, value_grads = [], []
    for c in range(CHUNKS):
        attended, query_grad, g_own, g_prev, g_rand, g_root = attention(
            info, queries, upstream, own, edge, root, rands[c], outs, c, chunk_heads
        )
        outs = (attended, query_grad)
        near = shifted(g_rand, "seq", -1)
        far = shifted(g_rand, "seq", -2)
        placed = place(wanted, g_rand, near, far, shard_blocks)
        summed = lax.psum_scatter(placed, "head", scatter_dimension=0, tiled=True)
        g_root = sum_to_first(sum_to_first(g_root, "seq"), "head")
        g_edge = shifted(g_prev[:1].astype(jnp.bfloat16), both, -1).astype(jnp.float32)
        total = g_own + summed.astype(jnp.float32)
        total = total + jnp.concatenate([g_prev[1:], g_edge], 0)
        head_of_row = jnp.where(is_first, g_root, 0.0)
        total = jnp.concatenate([total[:1] + head_of_row[None], total[1:]], 0)
        total = total.astype(jnp.bfloat16)
        key_grads.append(total[:, 0].reshape(tokens, chunk_width))
        value_grads.append(total[:, 1].reshape(tokens, chunk_width))
    return (
        outs[0],
        outs[1],
        jnp.concatenate(key_grads, 1),
        jnp.concatenate(value_grads, 1),
    )


def solution(mesh):
    tokens = P(("seq", "head"), None)
    return jax.shard_map(
        local,
        mesh=mesh,
        in_specs=(tokens, tokens, tokens, tokens, P("seq", None)),
        out_specs=(tokens, tokens, tokens, tokens),
        check_vma=False,
    )
```

```python
import functools
import math

import jax
import jax.numpy as jnp
from jax import lax
from jax.experimental import pallas as pl
from jax.experimental.pallas import tpu as pltpu
from jax.sharding import PartitionSpec as P

HEAD_SIZE = 128
BLOCK = 64
NEGATIVE = -1e30
CHUNKS = 2


def shifted(x, axis, by):
    length = lax.axis_size(axis)
    pairs = [(i, i + by) for i in range(length) if 0 <= i + by < length]
    return lax.ppermute(x, axis, pairs)


def attention_kernel(
    info, q_ref, up_ref, own_ref, before_ref, edge_ref, root_ref, rand_ref, *rest, groups, aliased
):
    if aliased:
        rest = rest[2:]
    att_ref, dq_ref, g_own, g_prev, g_rand, g_root = rest
    j = pl.program_id(1)
    scale = HEAD_SIZE ** (-0.5)
    first = info[0] + j == 0
    rows = groups * BLOCK
    q = jnp.concatenate(
        [q_ref[:, r * HEAD_SIZE : (r + 1) * HEAD_SIZE] for r in range(groups)], axis=0
    )
    up = jnp.concatenate(
        [up_ref[:, r * HEAD_SIZE : (r + 1) * HEAD_SIZE] for r in range(groups)], axis=0
    )
    prev = jnp.where(j == 0, edge_ref[0], before_ref[0])
    keys = jnp.concatenate([root_ref[0, 0], own_ref[0, 0], prev[0], rand_ref[0, 0]], axis=0)
    values = jnp.concatenate([root_ref[0, 1], own_ref[0, 1], prev[1], rand_ref[0, 1]], axis=0)
    up_t = up.T
    scores = lax.dot_general(
        keys, q, (((1,), (1,)), ((), ())), preferred_element_type=jnp.float32
    ) * (scale * math.log2(math.e))
    key_at = lax.broadcasted_iota(jnp.int32, (BLOCK, rows), 0)
    query_at = lax.broadcasted_iota(jnp.int32, (BLOCK, rows), 1) & (BLOCK - 1)
    causal = key_at <= query_at
    never = jnp.float32(NEGATIVE)
    zero = jnp.float32(0.0)
    root_off = jnp.where(causal, zero, jnp.where(first, never, zero))
    own_off = jnp.where(causal, jnp.where(first, never, zero), never)
    prev_off = jnp.where(info[1 + 2 * j] > 0, zero, never)
    rand_off = jnp.where(info[2 + 2 * j] > 0, zero, never)
    scores = jnp.concatenate(
        [
            scores[:BLOCK] + root_off,
            scores[BLOCK : 2 * BLOCK] + own_off,
            scores[2 * BLOCK : 3 * BLOCK] + prev_off,
            scores[3 * BLOCK :] + rand_off,
        ],
        axis=0,
    )
    top = jnp.max(scores, axis=0, keepdims=True)
    weights = jnp.exp2(scores - top)
    total = jnp.sum(weights, axis=0, keepdims=True)
    probs = (weights * (1.0 / total)).astype(jnp.bfloat16)
    att_t = lax.dot_general(
        values, probs, (((0,), (0,)), ((), ())), preferred_element_type=jnp.float32
    ).astype(jnp.bfloat16)
    delta = jnp.sum(
        att_t.astype(jnp.float32) * up_t.astype(jnp.float32), axis=0, keepdims=True
    )
    dprob = lax.dot_general(
        values, up_t, (((1,), (0,)), ((), ())), preferred_element_type=jnp.float32
    )
    dscore = (probs.astype(jnp.float32) * (dprob - delta)).astype(jnp.bfloat16)
    dq_t = lax.dot_general(
        keys, dscore, (((0,), (0,)), ((), ())), preferred_element_type=jnp.float32
    )
    dq = (dq_t * scale).astype(jnp.bfloat16).T
    att = att_t.T
    for r in range(groups):
        att_ref[:, r * HEAD_SIZE : (r + 1) * HEAD_SIZE] = att[r * BLOCK : (r + 1) * BLOCK]
        dq_ref[:, r * HEAD_SIZE : (r + 1) * HEAD_SIZE] = dq[r * BLOCK : (r + 1) * BLOCK]
    dkey = scale * jnp.dot(dscore, q, preferred_element_type=jnp.float32)
    dvalue = jnp.dot(probs, up, preferred_element_type=jnp.float32)
    g_own[0, 0] = dkey[BLOCK : 2 * BLOCK]
    g_own[0, 1] = dvalue[BLOCK : 2 * BLOCK]
    g_prev[0, 0] = dkey[2 * BLOCK : 3 * BLOCK]
    g_prev[0, 1] = dvalue[2 * BLOCK : 3 * BLOCK]
    g_rand[0, 0] = dkey[3 * BLOCK :].astype(jnp.bfloat16)
    g_rand[0, 1] = dvalue[3 * BLOCK :].astype(jnp.bfloat16)

    @pl.when(j == 0)
    def _():
        g_root[...] = jnp.zeros_like(g_root)

    g_root[0] += dkey[:BLOCK]
    g_root[1] += dvalue[:BLOCK]


def attention(info, queries, upstream, own, edge, root, rand, earlier, chunk, chunk_heads):
    blocks = own.shape[0]
    width = chunk_heads * HEAD_SIZE
    groups = queries.shape[1] // own.shape[3]
    wide = groups * HEAD_SIZE
    start = chunk * chunk_heads
    token_spec = pl.BlockSpec((BLOCK, wide), lambda g, j, _: (j, start + g))
    set_shape = (1, 2, BLOCK, HEAD_SIZE)
    in_specs = [
        token_spec,
        token_spec,
        pl.BlockSpec(set_shape, lambda g, j, _: (j, 0, 0, start + g)),
        pl.BlockSpec(set_shape, lambda g, j, _: (jnp.maximum(j - 1, 0), 0, 0, start + g)),
        pl.BlockSpec(set_shape, lambda g, j, _: (0, 0, 0, start + g)),
        pl.BlockSpec(set_shape, lambda g, j, _: (0, 0, 0, start + g)),
        pl.BlockSpec(set_shape, lambda g, j, _: (j, 0, 0, start + g)),
    ]
    operands = [queries, upstream, own, own, edge, root, rand]
    aliases = {}
    if earlier is not None:
        in_specs += [pl.BlockSpec(memory_space=pl.ANY)] * 2
        operands += list(earlier)
        aliases = {8: 0, 9: 1}
    by_block = pl.BlockSpec(set_shape, lambda g, j, _: (j, 0, 0, g))
    set_array = (blocks, 2, BLOCK, width)
    elements = blocks * chunk_heads * groups * BLOCK * 4 * BLOCK
    return pl.pallas_call(
        functools.partial(attention_kernel, groups=groups, aliased=earlier is not None),
        grid_spec=pltpu.PrefetchScalarGridSpec(
            num_scalar_prefetch=1,
            grid=(chunk_heads, blocks),
            in_specs=in_specs,
            out_specs=[
                token_spec,
                token_spec,
                by_block,
                by_block,
                by_block,
                pl.BlockSpec((2, BLOCK, HEAD_SIZE), lambda g, j, _: (0, 0, g)),
            ],
        ),
        out_shape=[
            jax.ShapeDtypeStruct(queries.shape, jnp.bfloat16),
            jax.ShapeDtypeStruct(queries.shape, jnp.bfloat16),
            jax.ShapeDtypeStruct(set_array, jnp.float32),
            jax.ShapeDtypeStruct(set_array, jnp.float32),
            jax.ShapeDtypeStruct(set_array, jnp.bfloat16),
            jax.ShapeDtypeStruct((2, BLOCK, width), jnp.float32),
        ],
        input_output_aliases=aliases,
        cost_estimate=pl.CostEstimate(
            flops=12 * elements * HEAD_SIZE,
            transcendentals=elements,
            bytes_accessed=blocks * chunk_heads * wide * BLOCK * 8,
        ),
        compiler_params=pltpu.CompilerParams(vmem_limit_bytes=40 * 1024 * 1024),
        name="attention",
    )(info, *operands)


def place_kernel(index, own_ref, near_ref, far_ref, out_ref, total):
    slots = own_ref.shape[0]
    count = out_ref.shape[0]
    total[...] = jnp.zeros_like(total)
    for part, ref in enumerate((own_ref, near_ref, far_ref)):
        for n in range(slots):
            at = index[part * slots + n]
            inside = jnp.logical_and(at >= 0, at < count)

            @pl.when(inside)
            def _(at=at, ref=ref, n=n):
                total[jnp.clip(at, 0, count - 1)] += ref[n].astype(jnp.float32)

    out_ref[...] = total[...].astype(jnp.bfloat16)


def place(index, own, near, far, count):
    slots, _, _, width = own.shape
    tile = 128
    spec = pl.BlockSpec((slots, 2, BLOCK, tile), lambda g, _: (0, 0, 0, g))
    return pl.pallas_call(
        place_kernel,
        grid_spec=pltpu.PrefetchScalarGridSpec(
            num_scalar_prefetch=1,
            grid=(width // tile,),
            in_specs=[spec] * 3,
            out_specs=pl.BlockSpec((count, 2, BLOCK, tile), lambda g, _: (0, 0, 0, g)),
            scratch_shapes=[pltpu.VMEM((count, 2, BLOCK, tile), jnp.float32)],
        ),
        out_shape=jax.ShapeDtypeStruct((count, 2, BLOCK, width), jnp.bfloat16),
        cost_estimate=pl.CostEstimate(
            flops=count * 2 * BLOCK * width,
            transcendentals=0,
            bytes_accessed=(3 * slots + count) * 2 * BLOCK * width * 2,
        ),
        name="place",
    )(index, own, near, far)


PIECES = 4


def tree_steps(length):
    steps, step = [], 1
    while step < length:
        steps.append(step)
        step *= 2
    return steps


def greet(head_steps, seq_steps, head_size, seq_size):
    shard, part = lax.axis_index("seq"), lax.axis_index("head")
    barrier = pltpu.get_barrier_semaphore()
    count = 0
    for axis, at, steps, length in (
        ("head", part, head_steps, head_size),
        ("seq", shard, seq_steps, seq_size),
    ):
        for step in steps:
            for other in (lax.rem(at + step, length), lax.rem(at + length - step, length)):
                pl.semaphore_signal(
                    barrier, inc=1, device_id={axis: other}, device_id_type=pl.DeviceIdType.MESH
                )
                count += 1
    pl.semaphore_wait(barrier, count)


def send(source, target, send_sem, recv_sem, axis, other):
    return pltpu.make_async_remote_copy(
        src_ref=source,
        dst_ref=target,
        send_sem=send_sem,
        recv_sem=recv_sem,
        device_id={axis: other},
        device_id_type=pl.DeviceIdType.MESH,
    )


def piece_of(c, width):
    half = width * 2 // PIECES
    return c // (PIECES // 2), pl.ds((c % (PIECES // 2)) * half, half)


def gather_kernel(
    head_size, seq_size, wanted, back, own, rand, root_out, *rest
):
    wholes, rest = rest[:PIECES], rest[PIECES:]
    (root, stage_near, stage_far, in_near, in_far,
     right_send, right_recv, left_send, left_recv, near_send, near_recv, far_send, far_recv,
     root_send, root_recv) = rest
    shard, part = lax.axis_index("seq"), lax.axis_index("head")
    blocks, _, _, width = own.shape
    count = wholes[0].shape[0]
    head_steps, seq_steps = tree_steps(head_size), tree_steps(seq_size)
    greet(head_steps, seq_steps, head_size, seq_size)
    right = jnp.minimum(part + 1, head_size - 1)
    left = jnp.maximum(part - 1, 0)
    for c in range(PIECES):
        kv, columns = piece_of(c, width)
        wholes[c][pl.ds(part * blocks, blocks)] = own[:, kv, :, columns]

    @pl.when(jnp.logical_and(shard == 0, part == 0))
    def _():
        root[...] = own[0]

    def piece(p, c):
        return wholes[c].at[pl.ds(p * blocks, blocks)]

    def going_right(k, c):
        p = jnp.maximum(part - k + 1, 0)
        return send(
            piece(p, c), piece(p, c), right_send.at[k, c], right_recv.at[k, c], "head", right
        )

    def going_left(k, c):
        p = jnp.minimum(part + k - 1, head_size - 1)
        return send(
            piece(p, c), piece(p, c), left_send.at[k, c], left_recv.at[k, c], "head", left
        )

    sends_right = lambda k: jnp.logical_and(part - k + 1 >= 0, part < head_size - 1)
    sends_left = lambda k: jnp.logical_and(part + k - 1 < head_size, part > 0)

    def arrivals(k, c):
        @pl.when(part - k >= 0)
        def _():
            going_right(k, c).wait_recv()

        @pl.when(part + k < head_size)
        def _():
            going_left(k, c).wait_recv()

    events = [("head", step) for step in head_steps] + [("seq", step) for step in seq_steps]

    def root_copy(e):
        axis, step = events[e]
        at, length = (part, head_size) if axis == "head" else (shard, seq_size)
        other = jnp.minimum(at + step, length - 1)
        copy = send(root, root, root_send.at[e], root_recv.at[e], axis, other)
        takes_part = shard == 0 if axis == "head" else shard >= 0
        gives = jnp.logical_and(takes_part, jnp.logical_and(at < step, at + step < length))
        gets = jnp.logical_and(takes_part, jnp.logical_and(at >= step, at < 2 * step))
        return copy, gives, gets

    def root_event(e):
        if 0 < e <= len(events):
            copy, _, gets = root_copy(e - 1)
            pl.when(gets)(copy.wait_recv)
        if e < len(events):
            copy, gives, _ = root_copy(e)
            pl.when(gives)(copy.start)

    done = 0
    for k in range(1, head_size):
        for c in range(PIECES):
            if k > 1:
                arrivals(k - 1, c)
            pl.when(sends_right(k))(going_right(k, c).start)
            pl.when(sends_left(k))(going_left(k, c).start)
            if c % 2 == 1:
                root_event(done)
                done += 1

    def near_copy(c):
        return send(
            stage_near.at[c], in_near.at[c], near_send.at[c], near_recv.at[c],
            "seq", jnp.minimum(shard + 1, seq_size - 1),
        )

    def far_copy(c):
        return send(
            stage_far.at[c], in_far.at[c], far_send.at[c], far_recv.at[c],
            "seq", jnp.minimum(shard + 2, seq_size - 1),
        )

    def block_at(n):
        return jnp.clip(wanted[n], 0, count - 1)

    for c in range(PIECES):
        arrivals(head_size - 1, c)
        for n in range(blocks):
            stage_far[c, n] = wholes[c][block_at(2 * blocks + n)]
        pl.when(shard + 2 < seq_size)(far_copy(c).start)
        for n in range(blocks):
            stage_near[c, n] = wholes[c][block_at(blocks + n)]
        pl.when(shard + 1 < seq_size)(near_copy(c).start)
        root_event(done)
        done += 1
    while done <= len(events):
        root_event(done)
        done += 1
    root_out[0] = root[...]
    for c in range(PIECES):
        kv, columns = piece_of(c, width)
        for n in range(blocks):
            rand[n, kv, :, columns] = wholes[c][block_at(n)]

        @pl.when(shard >= 1)
        def _(c=c, kv=kv, columns=columns):
            near_copy(c).wait_recv()
            for n in range(blocks):
                rand[n, kv, :, columns] = jnp.where(
                    back[n] == 1, in_near[c, n], rand[n, kv, :, columns]
                )

        @pl.when(shard >= 2)
        def _(c=c, kv=kv, columns=columns):
            far_copy(c).wait_recv()
            for n in range(blocks):
                rand[n, kv, :, columns] = jnp.where(
                    back[n] == 2, in_far[c, n], rand[n, kv, :, columns]
                )

    for c in range(PIECES):
        for k in range(1, head_size):
            pl.when(sends_right(k))(going_right(k, c).wait_send)
            pl.when(sends_left(k))(going_left(k, c).wait_send)
        pl.when(shard + 2 < seq_size)(far_copy(c).wait_send)
        pl.when(shard + 1 < seq_size)(near_copy(c).wait_send)
    for e in range(len(events)):
        copy, gives, _ = root_copy(e)
        pl.when(gives)(copy.wait_send)


def gather(wanted, back, own, head_size, seq_size):
    blocks, _, _, width = own.shape
    events = len(tree_steps(head_size)) + len(tree_steps(seq_size))
    half = width * 2 // PIECES
    vmem, smem = pltpu.MemorySpace.VMEM, pltpu.MemorySpace.SMEM
    moved = pltpu.VMEM((PIECES, blocks, BLOCK, half), jnp.bfloat16)
    line = pltpu.SemaphoreType.DMA((head_size, PIECES))
    hop = pltpu.SemaphoreType.DMA((PIECES,))
    return pl.pallas_call(
        functools.partial(gather_kernel, head_size, seq_size),
        in_specs=[
            pl.BlockSpec(memory_space=smem),
            pl.BlockSpec(memory_space=smem),
            pl.BlockSpec(memory_space=vmem),
        ],
        out_specs=[pl.BlockSpec(memory_space=vmem)] * 2,
        out_shape=[
            jax.ShapeDtypeStruct(own.shape, jnp.bfloat16),
            jax.ShapeDtypeStruct((1,) + own.shape[1:], jnp.bfloat16),
        ],
        scratch_shapes=[
            *[pltpu.VMEM((blocks * head_size, BLOCK, half), jnp.bfloat16)] * PIECES,
            pltpu.VMEM(own.shape[1:], jnp.bfloat16),
            moved, moved, moved, moved,
            line, line, line, line, hop, hop, hop, hop,
            pltpu.SemaphoreType.DMA((events,)),
            pltpu.SemaphoreType.DMA((events,)),
        ],
        compiler_params=pltpu.CompilerParams(
            collective_id=0, has_side_effects=True, vmem_limit_bytes=40 * 1024 * 1024
        ),
        name="gather",
    )(wanted, back, own)


def scatter_kernel(
    head_size, seq_size, *refs
):
    (placed, root_in, out, root_out, root, root_box, right_out, right_in, left_out, left_in,
     right_send, right_recv, left_send, left_recv, root_send, root_recv) = refs
    shard, part = lax.axis_index("seq"), lax.axis_index("head")
    blocks, _, _, width = out.shape
    head_steps, seq_steps = tree_steps(head_size), tree_steps(seq_size)
    greet(head_steps, seq_steps, head_size, seq_size)
    right = jnp.minimum(part + 1, head_size - 1)
    left = jnp.maximum(part - 1, 0)
    root[...] = root_in[...]

    def piece(p, c):
        kv, columns = piece_of(c, width)
        return placed.at[pl.ds(p * blocks, blocks), kv, :, columns]

    def going_right(d, c, source):
        return send(
            source, right_in.at[d, c], right_send.at[d, c], right_recv.at[d, c], "head", right
        )

    def going_left(d, c, source):
        return send(
            source, left_in.at[d, c], left_send.at[d, c], left_recv.at[d, c], "head", left
        )

    events = [("seq", step) for step in seq_steps[::-1]] + [
        ("head", step) for step in head_steps[::-1]
    ]

    def root_copy(e):
        axis, step = events[e]
        at, length = (part, head_size) if axis == "head" else (shard, seq_size)
        other = jnp.maximum(at - step, 0)
        copy = send(root, root_box.at[e], root_send.at[e], root_recv.at[e], axis, other)
        takes_part = shard == 0 if axis == "head" else shard >= 0
        gives = jnp.logical_and(takes_part, jnp.logical_and(at >= step, at < 2 * step))
        gets = jnp.logical_and(takes_part, jnp.logical_and(at < step, at + step < length))
        return copy, gives, gets

    def root_event(e):
        if 0 < e <= len(events):
            copy, _, gets = root_copy(e - 1)

            @pl.when(gets)
            def _():
                copy.wait_recv()
                root[...] += root_box[e - 1]

        if e < len(events):
            copy, gives, _ = root_copy(e)
            pl.when(gives)(copy.start)

    done = 0
    for k in range(1, head_size):
        to_right, to_left = head_size - k, k - 1
        for c in range(PIECES):

            @pl.when(part == 0)
            def _(d=to_right, c=c):
                going_right(d, c, piece(d, c)).start()

            @pl.when(jnp.logical_and(part > 0, part < to_right))
            def _(d=to_right, c=c):
                going_right(d, c, right_out.at[d, c]).wait_recv()
                right_out[d, c] = (
                    piece(d, c)[...].astype(jnp.float32) + right_in[d, c].astype(jnp.float32)
                ).astype(jnp.bfloat16)
                going_right(d, c, right_out.at[d, c]).start()

            @pl.when(part == head_size - 1)
            def _(d=to_left, c=c):
                going_left(d, c, piece(d, c)).start()

            @pl.when(jnp.logical_and(part < head_size - 1, part > to_left))
            def _(d=to_left, c=c):
                going_left(d, c, left_out.at[d, c]).wait_recv()
                left_out[d, c] = (
                    piece(d, c)[...].astype(jnp.float32) + left_in[d, c].astype(jnp.float32)
                ).astype(jnp.bfloat16)
                going_left(d, c, left_out.at[d, c]).start()

            if c % 2 == 1:
                root_event(done)
                done += 1
    while done <= len(events):
        root_event(done)
        done += 1
    for c in range(PIECES):
        kv, columns = piece_of(c, width)
        out[:, kv, :, columns] = piece(part, c)[...].astype(jnp.float32)

        @pl.when(part > 0)
        def _(c=c, kv=kv, columns=columns):
            going_right(part, c, right_out.at[part, c]).wait_recv()
            out[:, kv, :, columns] += right_in[part, c].astype(jnp.float32)

        @pl.when(part < head_size - 1)
        def _(c=c, kv=kv, columns=columns):
            going_left(part, c, left_out.at[part, c]).wait_recv()
            out[:, kv, :, columns] += left_in[part, c].astype(jnp.float32)

    root_out[...] = root[...]
    for d in range(head_size):
        for c in range(PIECES):
            pl.when(part < d)(going_right(d, c, right_out.at[d, c]).wait_send)
            pl.when(part > d)(going_left(d, c, left_out.at[d, c]).wait_send)
    for e in range(len(events)):
        copy, gives, _ = root_copy(e)
        pl.when(gives)(copy.wait_send)


def scatter(placed, root, head_size, seq_size):
    count, _, _, width = placed.shape
    blocks = count // head_size
    events = len(tree_steps(head_size)) + len(tree_steps(seq_size))
    half = width * 2 // PIECES
    vmem = pltpu.MemorySpace.VMEM
    box = pltpu.VMEM((head_size, PIECES, blocks, BLOCK, half), jnp.bfloat16)
    line = pltpu.SemaphoreType.DMA((head_size, PIECES))
    return pl.pallas_call(
        functools.partial(scatter_kernel, head_size, seq_size),
        in_specs=[pl.BlockSpec(memory_space=vmem)] * 2,
        out_specs=[pl.BlockSpec(memory_space=vmem)] * 2,
        out_shape=[
            jax.ShapeDtypeStruct((blocks,) + placed.shape[1:], jnp.float32),
            jax.ShapeDtypeStruct(root.shape, jnp.float32),
        ],
        scratch_shapes=[
            pltpu.VMEM(root.shape, jnp.float32),
            pltpu.VMEM((events,) + root.shape, jnp.float32),
            box, box, box, box,
            line, line, line, line,
            pltpu.SemaphoreType.DMA((events,)),
            pltpu.SemaphoreType.DMA((events,)),
        ],
        compiler_params=pltpu.CompilerParams(
            collective_id=1, has_side_effects=True, vmem_limit_bytes=48 * 1024 * 1024
        ),
        name="scatter",
    )(placed, root)


def local(queries, key_rows, value_rows, upstream, ancestors):
    tokens, width = key_rows.shape
    blocks = tokens // BLOCK
    shard_blocks = ancestors.shape[0]
    both = ("seq", "head")
    shard, part = lax.axis_index("seq"), lax.axis_index("head")
    origin = shard * shard_blocks
    mine = lax.dynamic_slice_in_dim(ancestors, part * blocks, blocks, 0)
    first_entry, last_entry = mine[:, 0], mine[:, 1]
    use_prev = first_entry >= 0
    use_rand = (last_entry >= 0) & (last_entry != first_entry)
    info = jnp.concatenate(
        [
            (origin + part * blocks)[None].astype(jnp.int32),
            jnp.stack([use_prev, use_rand], 1).reshape(-1).astype(jnp.int32),
        ]
    )
    wanted_near = shifted(last_entry, "seq", -1) - origin
    wanted_far = shifted(last_entry, "seq", -2) - origin
    wanted_own = last_entry - origin
    length = lax.axis_size("seq")
    wanted_near = jnp.where(shard + 1 < length, wanted_near, -1)
    wanted_far = jnp.where(shard + 2 < length, wanted_far, -1)
    wanted = jnp.concatenate([wanted_own, wanted_near, wanted_far]).astype(jnp.int32)

    own = jnp.stack(
        [key_rows.reshape(blocks, BLOCK, width), value_rows.reshape(blocks, BLOCK, width)], 1
    )
    chunk_heads = width // HEAD_SIZE // CHUNKS
    head_size, seq_size = lax.axis_size("head"), length
    is_first = (shard == 0) & (part == 0)
    edge = shifted(own[-1:], both, 1)
    back = (shard - last_entry // shard_blocks).astype(jnp.int32)
    rand, root = gather(wanted, back, own, head_size, seq_size)
    outs = None
    g_owns, g_prevs, placed, g_roots = [], [], [], []
    for c in range(CHUNKS):
        attended, query_grad, g_own, g_prev, g_rand, g_root = attention(
            info, queries, upstream, own, edge, root, rand, outs, c, chunk_heads
        )
        outs = (attended, query_grad)
        near = shifted(g_rand, "seq", -1)
        far = shifted(g_rand, "seq", -2)
        placed.append(place(wanted, g_rand, near, far, shard_blocks))
        g_owns.append(g_own)
        g_prevs.append(g_prev)
        g_roots.append(g_root)
    g_own, g_prev = jnp.concatenate(g_owns, -1), jnp.concatenate(g_prevs, -1)
    g_edge = shifted(g_prev[:1].astype(jnp.bfloat16), both, -1).astype(jnp.float32)
    summed, g_root = scatter(
        jnp.concatenate(placed, -1), jnp.concatenate(g_roots, -1), head_size, seq_size
    )
    total = g_own + summed + jnp.concatenate([g_prev[1:], g_edge], 0)
    head_of_row = jnp.where(is_first, g_root, 0.0)
    total = jnp.concatenate([total[:1] + head_of_row[None], total[1:]], 0)
    total = total.astype(jnp.bfloat16)
    return (
        outs[0],
        outs[1],
        total[:, 0].reshape(tokens, width),
        total[:, 1].reshape(tokens, width),
    )


def solution(mesh):
    tokens = P(("seq", "head"), None)
    return jax.shard_map(
        local,
        mesh=mesh,
        in_specs=(tokens, tokens, tokens, tokens, P("seq", None)),
        out_specs=(tokens, tokens, tokens, tokens),
        check_vma=False,
    )
```

```python
import functools
import math

import jax
import jax.numpy as jnp
from jax import lax
from jax.experimental import pallas as pl
from jax.experimental.pallas import tpu as pltpu
from jax.sharding import PartitionSpec as P

HEAD_SIZE = 128
BLOCK = 64
NEGATIVE = -1e30
CHUNKS = 2


def shifted(x, axis, by):
    length = lax.axis_size(axis)
    pairs = [(i, i + by) for i in range(length) if 0 <= i + by < length]
    return lax.ppermute(x, axis, pairs)


def attention_kernel(
    info, q_ref, up_ref, own_ref, before_ref, edge_ref, root_ref, rand_ref, *rest, groups, aliased
):
    if aliased:
        rest = rest[2:]
    att_ref, dq_ref, g_own, g_prev, g_rand, g_root = rest
    j = pl.program_id(1)
    scale = HEAD_SIZE ** (-0.5)
    first = info[0] + j == 0
    rows = groups * BLOCK
    q = jnp.concatenate(
        [q_ref[:, r * HEAD_SIZE : (r + 1) * HEAD_SIZE] for r in range(groups)], axis=0
    )
    up = jnp.concatenate(
        [up_ref[:, r * HEAD_SIZE : (r + 1) * HEAD_SIZE] for r in range(groups)], axis=0
    )
    prev = jnp.where(j == 0, edge_ref[0], before_ref[0])
    keys = jnp.concatenate([root_ref[0, 0], own_ref[0, 0], prev[0], rand_ref[0, 0]], axis=0)
    values = jnp.concatenate([root_ref[0, 1], own_ref[0, 1], prev[1], rand_ref[0, 1]], axis=0)
    up_t = up.T
    scores = lax.dot_general(
        keys, q, (((1,), (1,)), ((), ())), preferred_element_type=jnp.float32
    ) * (scale * math.log2(math.e))
    key_at = lax.broadcasted_iota(jnp.int32, (BLOCK, rows), 0)
    query_at = lax.broadcasted_iota(jnp.int32, (BLOCK, rows), 1) & (BLOCK - 1)
    causal = key_at <= query_at
    never = jnp.float32(NEGATIVE)
    zero = jnp.float32(0.0)
    root_off = jnp.where(causal, zero, jnp.where(first, never, zero))
    own_off = jnp.where(causal, jnp.where(first, never, zero), never)
    prev_off = jnp.where(info[1 + 2 * j] > 0, zero, never)
    rand_off = jnp.where(info[2 + 2 * j] > 0, zero, never)
    scores = jnp.concatenate(
        [
            scores[:BLOCK] + root_off,
            scores[BLOCK : 2 * BLOCK] + own_off,
            scores[2 * BLOCK : 3 * BLOCK] + prev_off,
            scores[3 * BLOCK :] + rand_off,
        ],
        axis=0,
    )
    top = jnp.max(scores, axis=0, keepdims=True)
    weights = jnp.exp2(scores - top)
    total = jnp.sum(weights, axis=0, keepdims=True)
    probs = (weights * (1.0 / total)).astype(jnp.bfloat16)
    att_t = lax.dot_general(
        values, probs, (((0,), (0,)), ((), ())), preferred_element_type=jnp.float32
    ).astype(jnp.bfloat16)
    delta = jnp.sum(
        att_t.astype(jnp.float32) * up_t.astype(jnp.float32), axis=0, keepdims=True
    )
    dprob = lax.dot_general(
        values, up_t, (((1,), (0,)), ((), ())), preferred_element_type=jnp.float32
    )
    dscore = (probs.astype(jnp.float32) * (dprob - delta)).astype(jnp.bfloat16)
    dq_t = lax.dot_general(
        keys, dscore, (((0,), (0,)), ((), ())), preferred_element_type=jnp.float32
    )
    dq = (dq_t * scale).astype(jnp.bfloat16).T
    att = att_t.T
    for r in range(groups):
        att_ref[:, r * HEAD_SIZE : (r + 1) * HEAD_SIZE] = att[r * BLOCK : (r + 1) * BLOCK]
        dq_ref[:, r * HEAD_SIZE : (r + 1) * HEAD_SIZE] = dq[r * BLOCK : (r + 1) * BLOCK]
    dkey = scale * jnp.dot(dscore, q, preferred_element_type=jnp.float32)
    dvalue = jnp.dot(probs, up, preferred_element_type=jnp.float32)
    g_own[0, 0] = dkey[BLOCK : 2 * BLOCK]
    g_own[0, 1] = dvalue[BLOCK : 2 * BLOCK]
    g_prev[0, 0] = dkey[2 * BLOCK : 3 * BLOCK]
    g_prev[0, 1] = dvalue[2 * BLOCK : 3 * BLOCK]
    g_rand[0, 0] = dkey[3 * BLOCK :].astype(jnp.bfloat16)
    g_rand[0, 1] = dvalue[3 * BLOCK :].astype(jnp.bfloat16)

    @pl.when(j == 0)
    def _():
        g_root[...] = jnp.zeros_like(g_root)

    g_root[0] += dkey[:BLOCK]
    g_root[1] += dvalue[:BLOCK]


def attention(info, queries, upstream, own, edge, root, rand, earlier, chunk, chunk_heads):
    blocks = own.shape[0]
    width = chunk_heads * HEAD_SIZE
    groups = queries.shape[1] // own.shape[3]
    wide = groups * HEAD_SIZE
    start = chunk * chunk_heads
    token_spec = pl.BlockSpec((BLOCK, wide), lambda g, j, _: (j, start + g))
    set_shape = (1, 2, BLOCK, HEAD_SIZE)
    in_specs = [
        token_spec,
        token_spec,
        pl.BlockSpec(set_shape, lambda g, j, _: (j, 0, 0, start + g)),
        pl.BlockSpec(set_shape, lambda g, j, _: (jnp.maximum(j - 1, 0), 0, 0, start + g)),
        pl.BlockSpec(set_shape, lambda g, j, _: (0, 0, 0, start + g)),
        pl.BlockSpec(set_shape, lambda g, j, _: (0, 0, 0, start + g)),
        pl.BlockSpec(set_shape, lambda g, j, _: (j, 0, 0, start + g)),
    ]
    operands = [queries, upstream, own, own, edge, root, rand]
    aliases = {}
    if earlier is not None:
        in_specs += [pl.BlockSpec(memory_space=pl.ANY)] * 2
        operands += list(earlier)
        aliases = {8: 0, 9: 1}
    by_block = pl.BlockSpec(set_shape, lambda g, j, _: (j, 0, 0, g))
    set_array = (blocks, 2, BLOCK, width)
    elements = blocks * chunk_heads * groups * BLOCK * 4 * BLOCK
    return pl.pallas_call(
        functools.partial(attention_kernel, groups=groups, aliased=earlier is not None),
        grid_spec=pltpu.PrefetchScalarGridSpec(
            num_scalar_prefetch=1,
            grid=(chunk_heads, blocks),
            in_specs=in_specs,
            out_specs=[
                token_spec,
                token_spec,
                by_block,
                by_block,
                by_block,
                pl.BlockSpec((2, BLOCK, HEAD_SIZE), lambda g, j, _: (0, 0, g)),
            ],
        ),
        out_shape=[
            jax.ShapeDtypeStruct(queries.shape, jnp.bfloat16),
            jax.ShapeDtypeStruct(queries.shape, jnp.bfloat16),
            jax.ShapeDtypeStruct(set_array, jnp.float32),
            jax.ShapeDtypeStruct(set_array, jnp.float32),
            jax.ShapeDtypeStruct(set_array, jnp.bfloat16),
            jax.ShapeDtypeStruct((2, BLOCK, width), jnp.float32),
        ],
        input_output_aliases=aliases,
        cost_estimate=pl.CostEstimate(
            flops=80 * elements * HEAD_SIZE,
            transcendentals=elements,
            bytes_accessed=blocks * chunk_heads * wide * BLOCK * 8,
        ),
        compiler_params=pltpu.CompilerParams(vmem_limit_bytes=40 * 1024 * 1024),
        name="attention",
    )(info, *operands)


def place_kernel(index, own_ref, near_ref, far_ref, out_ref, total):
    slots = own_ref.shape[0]
    count = out_ref.shape[0]
    total[...] = jnp.zeros_like(total)
    for part, ref in enumerate((own_ref, near_ref, far_ref)):
        for n in range(slots):
            at = index[part * slots + n]
            inside = jnp.logical_and(at >= 0, at < count)

            @pl.when(inside)
            def _(at=at, ref=ref, n=n):
                total[jnp.clip(at, 0, count - 1)] += ref[n].astype(jnp.float32)

    out_ref[...] = total[...].astype(jnp.bfloat16)


def place(index, own, near, far, count):
    slots, _, _, width = own.shape
    tile = 128
    spec = pl.BlockSpec((slots, 2, BLOCK, tile), lambda g, _: (0, 0, 0, g))
    return pl.pallas_call(
        place_kernel,
        grid_spec=pltpu.PrefetchScalarGridSpec(
            num_scalar_prefetch=1,
            grid=(width // tile,),
            in_specs=[spec] * 3,
            out_specs=pl.BlockSpec((count, 2, BLOCK, tile), lambda g, _: (0, 0, 0, g)),
            scratch_shapes=[pltpu.VMEM((count, 2, BLOCK, tile), jnp.float32)],
        ),
        out_shape=jax.ShapeDtypeStruct((count, 2, BLOCK, width), jnp.bfloat16),
        cost_estimate=pl.CostEstimate(
            flops=count * 2 * BLOCK * width,
            transcendentals=0,
            bytes_accessed=(3 * slots + count) * 2 * BLOCK * width * 2,
        ),
        name="place",
    )(index, own, near, far)


PIECES = 2 * CHUNKS


def tree_steps(length):
    steps, step = [], 1
    while step < length:
        steps.append(step)
        step *= 2
    return steps


def greet(head_steps, seq_steps, head_size, seq_size):
    shard, part = lax.axis_index("seq"), lax.axis_index("head")
    barrier = pltpu.get_barrier_semaphore()
    count = 0
    for axis, at, steps, length in (
        ("head", part, head_steps, head_size),
        ("seq", shard, seq_steps, seq_size),
    ):
        for step in steps:
            for other in (lax.rem(at + step, length), lax.rem(at + length - step, length)):
                pl.semaphore_signal(
                    barrier, inc=1, device_id={axis: other}, device_id_type=pl.DeviceIdType.MESH
                )
                count += 1
    pl.semaphore_wait(barrier, count)


def send(source, target, send_sem, recv_sem, axis, other):
    return pltpu.make_async_remote_copy(
        src_ref=source,
        dst_ref=target,
        send_sem=send_sem,
        recv_sem=recv_sem,
        device_id={axis: other},
        device_id_type=pl.DeviceIdType.MESH,
    )


def piece_of(c, width):
    half = width * 2 // PIECES
    return c // (PIECES // 2), pl.ds((c % (PIECES // 2)) * half, half)


def gather_kernel(
    head_size, seq_size, wanted, back, own, rand, root_out, *rest
):
    wholes, rest = rest[:PIECES], rest[PIECES:]
    (root, stage_near, stage_far, in_near, in_far,
     right_send, right_recv, left_send, left_recv, near_send, near_recv, far_send, far_recv,
     root_send, root_recv) = rest
    shard, part = lax.axis_index("seq"), lax.axis_index("head")
    blocks, _, _, width = own.shape
    count = wholes[0].shape[0]
    head_steps, seq_steps = tree_steps(head_size), tree_steps(seq_size)
    greet(head_steps, seq_steps, head_size, seq_size)
    right = jnp.minimum(part + 1, head_size - 1)
    left = jnp.maximum(part - 1, 0)
    for c in range(PIECES):
        kv, columns = piece_of(c, width)
        wholes[c][pl.ds(part * blocks, blocks)] = own[:, kv, :, columns]

    @pl.when(jnp.logical_and(shard == 0, part == 0))
    def _():
        root[...] = own[0]

    def piece(p, c):
        return wholes[c].at[pl.ds(p * blocks, blocks)]

    def going_right(k, c):
        p = jnp.maximum(part - k + 1, 0)
        return send(
            piece(p, c), piece(p, c), right_send.at[k, c], right_recv.at[k, c], "head", right
        )

    def going_left(k, c):
        p = jnp.minimum(part + k - 1, head_size - 1)
        return send(
            piece(p, c), piece(p, c), left_send.at[k, c], left_recv.at[k, c], "head", left
        )

    sends_right = lambda k: jnp.logical_and(part - k + 1 >= 0, part < head_size - 1)
    sends_left = lambda k: jnp.logical_and(part + k - 1 < head_size, part > 0)

    def arrivals(k, c):
        @pl.when(part - k >= 0)
        def _():
            going_right(k, c).wait_recv()

        @pl.when(part + k < head_size)
        def _():
            going_left(k, c).wait_recv()

    events = [("head", step) for step in head_steps] + [("seq", step) for step in seq_steps]

    def root_copy(e):
        axis, step = events[e]
        at, length = (part, head_size) if axis == "head" else (shard, seq_size)
        other = jnp.minimum(at + step, length - 1)
        copy = send(root, root, root_send.at[e], root_recv.at[e], axis, other)
        takes_part = shard == 0 if axis == "head" else shard >= 0
        gives = jnp.logical_and(takes_part, jnp.logical_and(at < step, at + step < length))
        gets = jnp.logical_and(takes_part, jnp.logical_and(at >= step, at < 2 * step))
        return copy, gives, gets

    def root_event(e):
        if 0 < e <= len(events):
            copy, _, gets = root_copy(e - 1)
            pl.when(gets)(copy.wait_recv)
        if e < len(events):
            copy, gives, _ = root_copy(e)
            pl.when(gives)(copy.start)

    done = 0
    for k in range(1, head_size):
        for c in range(PIECES):
            if k > 1:
                arrivals(k - 1, c)
            pl.when(sends_right(k))(going_right(k, c).start)
            pl.when(sends_left(k))(going_left(k, c).start)
            if c % 2 == 1:
                root_event(done)
                done += 1

    def near_copy(c):
        return send(
            stage_near.at[c], in_near.at[c], near_send.at[c], near_recv.at[c],
            "seq", jnp.minimum(shard + 1, seq_size - 1),
        )

    def far_copy(c):
        return send(
            stage_far.at[c], in_far.at[c], far_send.at[c], far_recv.at[c],
            "seq", jnp.minimum(shard + 2, seq_size - 1),
        )

    def block_at(n):
        return jnp.clip(wanted[n], 0, count - 1)

    for c in range(PIECES):
        arrivals(head_size - 1, c)
        for n in range(blocks):
            stage_far[c, n] = wholes[c][block_at(2 * blocks + n)]
        pl.when(shard + 2 < seq_size)(far_copy(c).start)
        for n in range(blocks):
            stage_near[c, n] = wholes[c][block_at(blocks + n)]
        pl.when(shard + 1 < seq_size)(near_copy(c).start)
        root_event(done)
        done += 1
    while done <= len(events):
        root_event(done)
        done += 1
    root_out[0] = root[...]
    for c in range(PIECES):
        kv, columns = piece_of(c, width)
        for n in range(blocks):
            rand[n, kv, :, columns] = wholes[c][block_at(n)]

        @pl.when(shard >= 1)
        def _(c=c, kv=kv, columns=columns):
            near_copy(c).wait_recv()
            for n in range(blocks):
                rand[n, kv, :, columns] = jnp.where(
                    back[n] == 1, in_near[c, n], rand[n, kv, :, columns]
                )

        @pl.when(shard >= 2)
        def _(c=c, kv=kv, columns=columns):
            far_copy(c).wait_recv()
            for n in range(blocks):
                rand[n, kv, :, columns] = jnp.where(
                    back[n] == 2, in_far[c, n], rand[n, kv, :, columns]
                )

    for c in range(PIECES):
        for k in range(1, head_size):
            pl.when(sends_right(k))(going_right(k, c).wait_send)
            pl.when(sends_left(k))(going_left(k, c).wait_send)
        pl.when(shard + 2 < seq_size)(far_copy(c).wait_send)
        pl.when(shard + 1 < seq_size)(near_copy(c).wait_send)
    for e in range(len(events)):
        copy, gives, _ = root_copy(e)
        pl.when(gives)(copy.wait_send)


def gather(wanted, back, own, head_size, seq_size):
    blocks, _, _, width = own.shape
    events = len(tree_steps(head_size)) + len(tree_steps(seq_size))
    half = width * 2 // PIECES
    vmem, smem = pltpu.MemorySpace.VMEM, pltpu.MemorySpace.SMEM
    moved = pltpu.VMEM((PIECES, blocks, BLOCK, half), jnp.bfloat16)
    line = pltpu.SemaphoreType.DMA((head_size, PIECES))
    hop = pltpu.SemaphoreType.DMA((PIECES,))
    return pl.pallas_call(
        functools.partial(gather_kernel, head_size, seq_size),
        in_specs=[
            pl.BlockSpec(memory_space=smem),
            pl.BlockSpec(memory_space=smem),
            pl.BlockSpec(memory_space=vmem),
        ],
        out_specs=[pl.BlockSpec(memory_space=vmem)] * 2,
        out_shape=[
            jax.ShapeDtypeStruct(own.shape, jnp.bfloat16),
            jax.ShapeDtypeStruct((1,) + own.shape[1:], jnp.bfloat16),
        ],
        scratch_shapes=[
            *[pltpu.VMEM((blocks * head_size, BLOCK, half), jnp.bfloat16)] * PIECES,
            pltpu.VMEM(own.shape[1:], jnp.bfloat16),
            moved, moved, moved, moved,
            line, line, line, line, hop, hop, hop, hop,
            pltpu.SemaphoreType.DMA((events,)),
            pltpu.SemaphoreType.DMA((events,)),
        ],
        compiler_params=pltpu.CompilerParams(
            collective_id=0, has_side_effects=True, vmem_limit_bytes=40 * 1024 * 1024
        ),
        name="gather",
    )(wanted, back, own)


def scatter_kernel(
    head_size, seq_size, *refs
):
    placed, refs = refs[:CHUNKS], refs[CHUNKS:]
    (root_in, out, root_out, root, root_box, right_out, right_in, left_out, left_in,
     right_send, right_recv, left_send, left_recv, root_send, root_recv) = refs
    shard, part = lax.axis_index("seq"), lax.axis_index("head")
    blocks, _, _, width = out.shape
    head_steps, seq_steps = tree_steps(head_size), tree_steps(seq_size)
    greet(head_steps, seq_steps, head_size, seq_size)
    right = jnp.minimum(part + 1, head_size - 1)
    left = jnp.maximum(part - 1, 0)
    root[...] = root_in[...]

    def piece(p, c):
        return placed[c % CHUNKS].at[pl.ds(p * blocks, blocks), c // CHUNKS]

    def going_right(d, c, source):
        return send(
            source, right_in.at[d, c], right_send.at[d, c], right_recv.at[d, c], "head", right
        )

    def going_left(d, c, source):
        return send(
            source, left_in.at[d, c], left_send.at[d, c], left_recv.at[d, c], "head", left
        )

    events = [("seq", step) for step in seq_steps[::-1]] + [
        ("head", step) for step in head_steps[::-1]
    ]

    def root_copy(e):
        axis, step = events[e]
        at, length = (part, head_size) if axis == "head" else (shard, seq_size)
        other = jnp.maximum(at - step, 0)
        copy = send(root, root_box.at[e], root_send.at[e], root_recv.at[e], axis, other)
        takes_part = shard == 0 if axis == "head" else shard >= 0
        gives = jnp.logical_and(takes_part, jnp.logical_and(at >= step, at < 2 * step))
        gets = jnp.logical_and(takes_part, jnp.logical_and(at < step, at + step < length))
        return copy, gives, gets

    def root_event(e):
        if 0 < e <= len(events):
            copy, _, gets = root_copy(e - 1)

            @pl.when(gets)
            def _():
                copy.wait_recv()
                root[...] += root_box[e - 1]

        if e < len(events):
            copy, gives, _ = root_copy(e)
            pl.when(gives)(copy.start)

    done = 0
    for k in range(1, head_size):
        to_right, to_left = head_size - k, k - 1
        for c in range(PIECES):

            @pl.when(part == 0)
            def _(d=to_right, c=c):
                going_right(d, c, piece(d, c)).start()

            @pl.when(jnp.logical_and(part > 0, part < to_right))
            def _(d=to_right, c=c):
                going_right(d, c, right_out.at[d, c]).wait_recv()
                right_out[d, c] = (
                    piece(d, c)[...].astype(jnp.float32) + right_in[d, c].astype(jnp.float32)
                ).astype(jnp.bfloat16)
                going_right(d, c, right_out.at[d, c]).start()

            @pl.when(part == head_size - 1)
            def _(d=to_left, c=c):
                going_left(d, c, piece(d, c)).start()

            @pl.when(jnp.logical_and(part < head_size - 1, part > to_left))
            def _(d=to_left, c=c):
                going_left(d, c, left_out.at[d, c]).wait_recv()
                left_out[d, c] = (
                    piece(d, c)[...].astype(jnp.float32) + left_in[d, c].astype(jnp.float32)
                ).astype(jnp.bfloat16)
                going_left(d, c, left_out.at[d, c]).start()

            root_event(done)
            done += 1
    while done <= len(events):
        root_event(done)
        done += 1
    for c in range(PIECES):
        kv, columns = piece_of(c, width)
        out[:, kv, :, columns] = piece(part, c)[...].astype(jnp.float32)

        @pl.when(part > 0)
        def _(c=c, kv=kv, columns=columns):
            going_right(part, c, right_out.at[part, c]).wait_recv()
            out[:, kv, :, columns] += right_in[part, c].astype(jnp.float32)

        @pl.when(part < head_size - 1)
        def _(c=c, kv=kv, columns=columns):
            going_left(part, c, left_out.at[part, c]).wait_recv()
            out[:, kv, :, columns] += left_in[part, c].astype(jnp.float32)

    root_out[...] = root[...]
    for d in range(head_size):
        for c in range(PIECES):
            pl.when(part < d)(going_right(d, c, right_out.at[d, c]).wait_send)
            pl.when(part > d)(going_left(d, c, left_out.at[d, c]).wait_send)
    for e in range(len(events)):
        copy, gives, _ = root_copy(e)
        pl.when(gives)(copy.wait_send)


def scatter(placed, root, head_size, seq_size):
    count = placed[0].shape[0]
    width = root.shape[-1]
    blocks = count // head_size
    events = len(tree_steps(head_size)) + len(tree_steps(seq_size))
    half = width * 2 // PIECES
    vmem = pltpu.MemorySpace.VMEM
    box = pltpu.VMEM((head_size, PIECES, blocks, BLOCK, half), jnp.bfloat16)
    line = pltpu.SemaphoreType.DMA((head_size, PIECES))
    return pl.pallas_call(
        functools.partial(scatter_kernel, head_size, seq_size),
        in_specs=[pl.BlockSpec(memory_space=vmem)] * (CHUNKS + 1),
        out_specs=[pl.BlockSpec(memory_space=vmem)] * 2,
        out_shape=[
            jax.ShapeDtypeStruct((blocks, 2, BLOCK, width), jnp.float32),
            jax.ShapeDtypeStruct(root.shape, jnp.float32),
        ],
        scratch_shapes=[
            pltpu.VMEM(root.shape, jnp.float32),
            pltpu.VMEM((events,) + root.shape, jnp.float32),
            box, box, box, box,
            line, line, line, line,
            pltpu.SemaphoreType.DMA((events,)),
            pltpu.SemaphoreType.DMA((events,)),
        ],
        compiler_params=pltpu.CompilerParams(
            collective_id=1, has_side_effects=True, vmem_limit_bytes=48 * 1024 * 1024
        ),
        name="scatter",
    )(*placed, root)


def local(queries, key_rows, value_rows, upstream, ancestors):
    tokens, width = key_rows.shape
    blocks = tokens // BLOCK
    shard_blocks = ancestors.shape[0]
    both = ("seq", "head")
    shard, part = lax.axis_index("seq"), lax.axis_index("head")
    origin = shard * shard_blocks
    mine = lax.dynamic_slice_in_dim(ancestors, part * blocks, blocks, 0)
    first_entry, last_entry = mine[:, 0], mine[:, 1]
    use_prev = first_entry >= 0
    use_rand = (last_entry >= 0) & (last_entry != first_entry)
    info = jnp.concatenate(
        [
            (origin + part * blocks)[None].astype(jnp.int32),
            jnp.stack([use_prev, use_rand], 1).reshape(-1).astype(jnp.int32),
        ]
    )
    wanted_near = shifted(last_entry, "seq", -1) - origin
    wanted_far = shifted(last_entry, "seq", -2) - origin
    wanted_own = last_entry - origin
    length = lax.axis_size("seq")
    wanted_near = jnp.where(shard + 1 < length, wanted_near, -1)
    wanted_far = jnp.where(shard + 2 < length, wanted_far, -1)
    wanted = jnp.concatenate([wanted_own, wanted_near, wanted_far]).astype(jnp.int32)

    own = jnp.stack(
        [key_rows.reshape(blocks, BLOCK, width), value_rows.reshape(blocks, BLOCK, width)], 1
    )
    chunk_heads = width // HEAD_SIZE // CHUNKS
    head_size, seq_size = lax.axis_size("head"), length
    is_first = (shard == 0) & (part == 0)
    edge = shifted(own[-1:], both, 1)
    back = (shard - last_entry // shard_blocks).astype(jnp.int32)
    rand, root = gather(wanted, back, own, head_size, seq_size)
    outs = None
    g_owns, g_prevs, placed, g_roots = [], [], [], []
    for c in range(CHUNKS):
        attended, query_grad, g_own, g_prev, g_rand, g_root = attention(
            info, queries, upstream, own, edge, root, rand, outs, c, chunk_heads
        )
        outs = (attended, query_grad)
        near = shifted(g_rand, "seq", -1)
        far = shifted(g_rand, "seq", -2)
        placed.append(place(wanted, g_rand, near, far, shard_blocks))
        g_owns.append(g_own)
        g_prevs.append(g_prev)
        g_roots.append(g_root)
    g_own, g_prev = jnp.concatenate(g_owns, -1), jnp.concatenate(g_prevs, -1)
    g_edge = shifted(g_prev[:1].astype(jnp.bfloat16), both, -1).astype(jnp.float32)
    summed, g_root = scatter(
        placed, jnp.concatenate(g_roots, -1), head_size, seq_size
    )
    total = g_own + summed + jnp.concatenate([g_prev[1:], g_edge], 0)
    head_of_row = jnp.where(is_first, g_root, 0.0)
    total = jnp.concatenate([total[:1] + head_of_row[None], total[1:]], 0)
    total = total.astype(jnp.bfloat16)
    return (
        outs[0],
        outs[1],
        total[:, 0].reshape(tokens, width),
        total[:, 1].reshape(tokens, width),
    )


def solution(mesh):
    tokens = P(("seq", "head"), None)
    return jax.shard_map(
        local,
        mesh=mesh,
        in_specs=(tokens, tokens, tokens, tokens, P("seq", None)),
        out_specs=(tokens, tokens, tokens, tokens),
        check_vma=False,
    )
```

```python
import functools
import math

import jax
import jax.numpy as jnp
from jax import lax
from jax.experimental import pallas as pl
from jax.experimental.pallas import tpu as pltpu
from jax.sharding import PartitionSpec as P

HEAD_SIZE = 128
BLOCK = 64
NEGATIVE = -1e30
CHUNKS = 2


def shifted(x, axis, by):
    length = lax.axis_size(axis)
    pairs = [(i, i + by) for i in range(length) if 0 <= i + by < length]
    return lax.ppermute(x, axis, pairs)


def attention_kernel(
    info, q_ref, up_ref, own_ref, before_ref, edge_ref, root_ref, rand_ref, *rest, groups, aliased
):
    if aliased:
        rest = rest[2:]
    att_ref, dq_ref, g_own, g_prev, g_rand, g_root = rest
    j = pl.program_id(1)
    scale = HEAD_SIZE ** (-0.5)
    first = info[0] + j == 0
    rows = groups * BLOCK
    q = jnp.concatenate(
        [q_ref[:, r * HEAD_SIZE : (r + 1) * HEAD_SIZE] for r in range(groups)], axis=0
    )
    up = jnp.concatenate(
        [up_ref[:, r * HEAD_SIZE : (r + 1) * HEAD_SIZE] for r in range(groups)], axis=0
    )
    prev = jnp.where(j == 0, edge_ref[0], before_ref[0])
    keys = jnp.concatenate([root_ref[0, 0], own_ref[0, 0], prev[0], rand_ref[0, 0]], axis=0)
    values = jnp.concatenate([root_ref[0, 1], own_ref[0, 1], prev[1], rand_ref[0, 1]], axis=0)
    up_t = up.T
    scores = lax.dot_general(
        keys, q, (((1,), (1,)), ((), ())), preferred_element_type=jnp.float32
    ) * (scale * math.log2(math.e))
    key_at = lax.broadcasted_iota(jnp.int32, (BLOCK, rows), 0)
    query_at = lax.broadcasted_iota(jnp.int32, (BLOCK, rows), 1) & (BLOCK - 1)
    causal = key_at <= query_at
    never = jnp.float32(NEGATIVE)
    zero = jnp.float32(0.0)
    root_off = jnp.where(causal, zero, jnp.where(first, never, zero))
    own_off = jnp.where(causal, jnp.where(first, never, zero), never)
    prev_off = jnp.where(info[1 + 2 * j] > 0, zero, never)
    rand_off = jnp.where(info[2 + 2 * j] > 0, zero, never)
    scores = jnp.concatenate(
        [
            scores[:BLOCK] + root_off,
            scores[BLOCK : 2 * BLOCK] + own_off,
            scores[2 * BLOCK : 3 * BLOCK] + prev_off,
            scores[3 * BLOCK :] + rand_off,
        ],
        axis=0,
    )
    top = jnp.max(scores, axis=0, keepdims=True)
    weights = jnp.exp2(scores - top)
    total = jnp.sum(weights, axis=0, keepdims=True)
    probs = (weights * (1.0 / total)).astype(jnp.bfloat16)
    att_t = lax.dot_general(
        values, probs, (((0,), (0,)), ((), ())), preferred_element_type=jnp.float32
    ).astype(jnp.bfloat16)
    delta = jnp.sum(
        att_t.astype(jnp.float32) * up_t.astype(jnp.float32), axis=0, keepdims=True
    )
    dprob = lax.dot_general(
        values, up_t, (((1,), (0,)), ((), ())), preferred_element_type=jnp.float32
    )
    dscore = (probs.astype(jnp.float32) * (dprob - delta)).astype(jnp.bfloat16)
    dq_t = lax.dot_general(
        keys, dscore, (((0,), (0,)), ((), ())), preferred_element_type=jnp.float32
    )
    dq = (dq_t * scale).astype(jnp.bfloat16).T
    att = att_t.T
    for r in range(groups):
        att_ref[:, r * HEAD_SIZE : (r + 1) * HEAD_SIZE] = att[r * BLOCK : (r + 1) * BLOCK]
        dq_ref[:, r * HEAD_SIZE : (r + 1) * HEAD_SIZE] = dq[r * BLOCK : (r + 1) * BLOCK]
    dkey = scale * jnp.dot(dscore, q, preferred_element_type=jnp.float32)
    dvalue = jnp.dot(probs, up, preferred_element_type=jnp.float32)
    g_own[0, 0] = dkey[BLOCK : 2 * BLOCK]
    g_own[0, 1] = dvalue[BLOCK : 2 * BLOCK]
    g_prev[0, 0] = dkey[2 * BLOCK : 3 * BLOCK]
    g_prev[0, 1] = dvalue[2 * BLOCK : 3 * BLOCK]
    g_rand[0, 0] = dkey[3 * BLOCK :].astype(jnp.bfloat16)
    g_rand[0, 1] = dvalue[3 * BLOCK :].astype(jnp.bfloat16)

    @pl.when(j == 0)
    def _():
        g_root[...] = jnp.zeros_like(g_root)

    g_root[0] += dkey[:BLOCK]
    g_root[1] += dvalue[:BLOCK]


def attention(info, queries, upstream, own, edge, root, rand, earlier, chunk, chunk_heads):
    blocks = own.shape[0]
    width = chunk_heads * HEAD_SIZE
    groups = queries.shape[1] // own.shape[3]
    wide = groups * HEAD_SIZE
    start = chunk * chunk_heads
    token_spec = pl.BlockSpec((BLOCK, wide), lambda g, j, _: (j, start + g))
    set_shape = (1, 2, BLOCK, HEAD_SIZE)
    in_specs = [
        token_spec,
        token_spec,
        pl.BlockSpec(set_shape, lambda g, j, _: (j, 0, 0, start + g)),
        pl.BlockSpec(set_shape, lambda g, j, _: (jnp.maximum(j - 1, 0), 0, 0, start + g)),
        pl.BlockSpec(set_shape, lambda g, j, _: (0, 0, 0, start + g)),
        pl.BlockSpec(set_shape, lambda g, j, _: (0, 0, 0, start + g)),
        pl.BlockSpec(set_shape, lambda g, j, _: (j, 0, 0, start + g)),
    ]
    operands = [queries, upstream, own, own, edge, root, rand]
    aliases = {}
    if earlier is not None:
        in_specs += [pl.BlockSpec(memory_space=pl.ANY)] * 2
        operands += list(earlier)
        aliases = {8: 0, 9: 1}
    by_block = pl.BlockSpec(set_shape, lambda g, j, _: (j, 0, 0, g))
    set_array = (blocks, 2, BLOCK, width)
    elements = blocks * chunk_heads * groups * BLOCK * 4 * BLOCK
    return pl.pallas_call(
        functools.partial(attention_kernel, groups=groups, aliased=earlier is not None),
        grid_spec=pltpu.PrefetchScalarGridSpec(
            num_scalar_prefetch=1,
            grid=(chunk_heads, blocks),
            in_specs=in_specs,
            out_specs=[
                token_spec,
                token_spec,
                by_block,
                by_block,
                by_block,
                pl.BlockSpec((2, BLOCK, HEAD_SIZE), lambda g, j, _: (0, 0, g)),
            ],
        ),
        out_shape=[
            jax.ShapeDtypeStruct(queries.shape, jnp.bfloat16),
            jax.ShapeDtypeStruct(queries.shape, jnp.bfloat16),
            jax.ShapeDtypeStruct(set_array, jnp.float32),
            jax.ShapeDtypeStruct(set_array, jnp.float32),
            jax.ShapeDtypeStruct(set_array, jnp.bfloat16),
            jax.ShapeDtypeStruct((2, BLOCK, width), jnp.float32),
        ],
        input_output_aliases=aliases,
        cost_estimate=pl.CostEstimate(
            flops=80 * elements * HEAD_SIZE,
            transcendentals=elements,
            bytes_accessed=blocks * chunk_heads * wide * BLOCK * 8,
        ),
        compiler_params=pltpu.CompilerParams(vmem_limit_bytes=40 * 1024 * 1024),
        name="attention",
    )(info, *operands)


def place_kernel(index, own_ref, near_ref, far_ref, out_ref, total):
    slots = own_ref.shape[0]
    count = out_ref.shape[0]
    total[...] = jnp.zeros_like(total)
    for part, ref in enumerate((own_ref, near_ref, far_ref)):
        for n in range(slots):
            at = index[part * slots + n]
            inside = jnp.logical_and(at >= 0, at < count)

            @pl.when(inside)
            def _(at=at, ref=ref, n=n):
                total[jnp.clip(at, 0, count - 1)] += ref[n].astype(jnp.float32)

    out_ref[...] = total[...].astype(jnp.bfloat16)


def place(index, own, near, far, count):
    slots, _, _, width = own.shape
    tile = 128
    spec = pl.BlockSpec((slots, 2, BLOCK, tile), lambda g, _: (0, 0, 0, g))
    return pl.pallas_call(
        place_kernel,
        grid_spec=pltpu.PrefetchScalarGridSpec(
            num_scalar_prefetch=1,
            grid=(width // tile,),
            in_specs=[spec] * 3,
            out_specs=pl.BlockSpec((count, 2, BLOCK, tile), lambda g, _: (0, 0, 0, g)),
            scratch_shapes=[pltpu.VMEM((count, 2, BLOCK, tile), jnp.float32)],
        ),
        out_shape=jax.ShapeDtypeStruct((count, 2, BLOCK, width), jnp.bfloat16),
        cost_estimate=pl.CostEstimate(
            flops=count * 2 * BLOCK * width,
            transcendentals=0,
            bytes_accessed=(3 * slots + count) * 2 * BLOCK * width * 2,
        ),
        name="place",
    )(index, own, near, far)


PIECES = 2 * CHUNKS


def tree_steps(length):
    steps, step = [], 1
    while step < length:
        steps.append(step)
        step *= 2
    return steps


def greet(head_steps, seq_steps, head_size, seq_size):
    shard, part = lax.axis_index("seq"), lax.axis_index("head")
    barrier = pltpu.get_barrier_semaphore()
    count = 0
    for axis, at, steps, length in (
        ("head", part, head_steps, head_size),
        ("seq", shard, seq_steps, seq_size),
    ):
        for step in steps:
            for other in (lax.rem(at + step, length), lax.rem(at + length - step, length)):
                pl.semaphore_signal(
                    barrier, inc=1, device_id={axis: other}, device_id_type=pl.DeviceIdType.MESH
                )
                count += 1
    pl.semaphore_wait(barrier, count)


def send(source, target, send_sem, recv_sem, axis, other):
    return pltpu.make_async_remote_copy(
        src_ref=source,
        dst_ref=target,
        send_sem=send_sem,
        recv_sem=recv_sem,
        device_id={axis: other},
        device_id_type=pl.DeviceIdType.MESH,
    )


def piece_of(c, width):
    half = width * 2 // PIECES
    return c // (PIECES // 2), pl.ds((c % (PIECES // 2)) * half, half)


def gather_kernel(
    head_size, seq_size, wanted, back, own, rand, root_out, *rest
):
    wholes, rest = rest[:PIECES], rest[PIECES:]
    (root, stage_near, stage_far, in_near, in_far,
     right_send, right_recv, left_send, left_recv, near_send, near_recv, far_send, far_recv,
     root_send, root_recv) = rest
    shard, part = lax.axis_index("seq"), lax.axis_index("head")
    blocks, _, _, width = own.shape
    count = wholes[0].shape[0]
    seq_steps = tree_steps(seq_size)
    greet(range(1, head_size // 2 + 1), seq_steps, head_size, seq_size)
    right = jnp.minimum(part + 1, head_size - 1)
    left = jnp.maximum(part - 1, 0)
    for c in range(PIECES):
        kv, columns = piece_of(c, width)
        wholes[c][pl.ds(part * blocks, blocks)] = own[:, kv, :, columns]

    @pl.when(jnp.logical_and(shard == 0, part == 0))
    def _():
        root[...] = own[0]

    def piece(p, c):
        return wholes[c].at[pl.ds(p * blocks, blocks)]

    def going_right(k, c):
        p = jnp.maximum(part - k + 1, 0)
        return send(
            piece(p, c), piece(p, c), right_send.at[k, c], right_recv.at[k, c], "head", right
        )

    def going_left(k, c):
        p = jnp.minimum(part + k - 1, head_size - 1)
        return send(
            piece(p, c), piece(p, c), left_send.at[k, c], left_recv.at[k, c], "head", left
        )

    sends_right = lambda k: jnp.logical_and(part - k + 1 >= 0, part < head_size - 1)
    sends_left = lambda k: jnp.logical_and(part + k - 1 < head_size, part > 0)

    def arrivals(k, c):
        @pl.when(part - k >= 0)
        def _():
            going_right(k, c).wait_recv()

        @pl.when(part + k < head_size)
        def _():
            going_left(k, c).wait_recv()

    def root_over_head(z):
        return send(root, root, root_send.at[z - 1], root_recv.at[z - 1], "head", z)

    def root_over_seq(e):
        step = seq_steps[e]
        other = jnp.minimum(shard + step, seq_size - 1)
        at = head_size - 1 + e
        copy = send(root, root, root_send.at[at], root_recv.at[at], "seq", other)
        gives = jnp.logical_and(shard < step, shard + step < seq_size)
        gets = jnp.logical_and(shard >= step, shard < 2 * step)
        return copy, gives, gets

    at_first = jnp.logical_and(shard == 0, part == 0)

    @pl.when(at_first)
    def _():
        for z in range(1, head_size):
            root_over_head(z).start()

    def root_event(e):
        if e == 0:

            @pl.when(jnp.logical_and(shard == 0, part > 0))
            def _():
                root_over_head(jnp.maximum(part, 1)).wait_recv()

        elif e <= len(seq_steps):
            copy, _, gets = root_over_seq(e - 1)
            pl.when(gets)(copy.wait_recv)
        if e < len(seq_steps):
            copy, gives, _ = root_over_seq(e)
            pl.when(gives)(copy.start)

    done = 0
    for k in range(1, head_size):
        for c in range(PIECES):
            if k > 1:
                arrivals(k - 1, c)
            pl.when(sends_right(k))(going_right(k, c).start)
            pl.when(sends_left(k))(going_left(k, c).start)
            if c % 2 == 1:
                root_event(done)
                done += 1

    def near_copy(c):
        return send(
            stage_near.at[c], in_near.at[c], near_send.at[c], near_recv.at[c],
            "seq", jnp.minimum(shard + 1, seq_size - 1),
        )

    def far_copy(c):
        return send(
            stage_far.at[c], in_far.at[c], far_send.at[c], far_recv.at[c],
            "seq", jnp.minimum(shard + 2, seq_size - 1),
        )

    def block_at(n):
        return jnp.clip(wanted[n], 0, count - 1)

    for c in range(PIECES):
        arrivals(head_size - 1, c)
        for n in range(blocks):
            stage_far[c, n] = wholes[c][block_at(2 * blocks + n)]
        pl.when(shard + 2 < seq_size)(far_copy(c).start)
        for n in range(blocks):
            stage_near[c, n] = wholes[c][block_at(blocks + n)]
        pl.when(shard + 1 < seq_size)(near_copy(c).start)
    while done <= len(seq_steps):
        root_event(done)
        done += 1
    root_out[0] = root[...]
    for c in range(PIECES):
        kv, columns = piece_of(c, width)
        for n in range(blocks):
            rand[n, kv, :, columns] = wholes[c][block_at(n)]

        @pl.when(shard >= 1)
        def _(c=c, kv=kv, columns=columns):
            near_copy(c).wait_recv()
            for n in range(blocks):
                rand[n, kv, :, columns] = jnp.where(
                    back[n] == 1, in_near[c, n], rand[n, kv, :, columns]
                )

        @pl.when(shard >= 2)
        def _(c=c, kv=kv, columns=columns):
            far_copy(c).wait_recv()
            for n in range(blocks):
                rand[n, kv, :, columns] = jnp.where(
                    back[n] == 2, in_far[c, n], rand[n, kv, :, columns]
                )

    for c in range(PIECES):
        for k in range(1, head_size):
            pl.when(sends_right(k))(going_right(k, c).wait_send)
            pl.when(sends_left(k))(going_left(k, c).wait_send)
        pl.when(shard + 2 < seq_size)(far_copy(c).wait_send)
        pl.when(shard + 1 < seq_size)(near_copy(c).wait_send)
    for e in range(len(seq_steps)):
        copy, gives, _ = root_over_seq(e)
        pl.when(gives)(copy.wait_send)

    @pl.when(at_first)
    def _():
        for z in range(1, head_size):
            root_over_head(z).wait_send()


def gather(wanted, back, own, head_size, seq_size):
    blocks, _, _, width = own.shape
    events = head_size - 1 + len(tree_steps(seq_size))
    half = width * 2 // PIECES
    vmem, smem = pltpu.MemorySpace.VMEM, pltpu.MemorySpace.SMEM
    moved = pltpu.VMEM((PIECES, blocks, BLOCK, half), jnp.bfloat16)
    line = pltpu.SemaphoreType.DMA((head_size, PIECES))
    hop = pltpu.SemaphoreType.DMA((PIECES,))
    return pl.pallas_call(
        functools.partial(gather_kernel, head_size, seq_size),
        in_specs=[
            pl.BlockSpec(memory_space=smem),
            pl.BlockSpec(memory_space=smem),
            pl.BlockSpec(memory_space=vmem),
        ],
        out_specs=[pl.BlockSpec(memory_space=vmem)] * 2,
        out_shape=[
            jax.ShapeDtypeStruct(own.shape, jnp.bfloat16),
            jax.ShapeDtypeStruct((1,) + own.shape[1:], jnp.bfloat16),
        ],
        scratch_shapes=[
            *[pltpu.VMEM((blocks * head_size, BLOCK, half), jnp.bfloat16)] * PIECES,
            pltpu.VMEM(own.shape[1:], jnp.bfloat16),
            moved, moved, moved, moved,
            line, line, line, line, hop, hop, hop, hop,
            pltpu.SemaphoreType.DMA((events,)),
            pltpu.SemaphoreType.DMA((events,)),
        ],
        compiler_params=pltpu.CompilerParams(
            collective_id=0, has_side_effects=True, vmem_limit_bytes=40 * 1024 * 1024
        ),
        name="gather",
    )(wanted, back, own)


def scatter_kernel(
    head_size, seq_size, *refs
):
    placed, refs = refs[:CHUNKS], refs[CHUNKS:]
    (root_in, out, root_out, root, root_box, right_out, right_in, left_out, left_in,
     right_send, right_recv, left_send, left_recv, root_send, root_recv) = refs
    shard, part = lax.axis_index("seq"), lax.axis_index("head")
    blocks, _, _, width = out.shape
    seq_steps = tree_steps(seq_size)
    greet(range(1, head_size // 2 + 1), seq_steps, head_size, seq_size)
    right = jnp.minimum(part + 1, head_size - 1)
    left = jnp.maximum(part - 1, 0)
    root[...] = root_in[...]

    def piece(p, c):
        return placed[c % CHUNKS].at[pl.ds(p * blocks, blocks), c // CHUNKS]

    def going_right(d, c, source):
        return send(
            source, right_in.at[d, c], right_send.at[d, c], right_recv.at[d, c], "head", right
        )

    def going_left(d, c, source):
        return send(
            source, left_in.at[d, c], left_send.at[d, c], left_recv.at[d, c], "head", left
        )

    seq_steps = seq_steps[::-1]

    def root_over_seq(e):
        step = seq_steps[e]
        other = jnp.maximum(shard - step, 0)
        at = head_size - 1 + e
        copy = send(root, root_box.at[at], root_send.at[at], root_recv.at[at], "seq", other)
        gives = jnp.logical_and(shard >= step, shard < 2 * step)
        gets = jnp.logical_and(shard < step, shard + step < seq_size)
        return copy, gives, gets

    def root_over_head(z):
        return send(
            root, root_box.at[z - 1], root_send.at[z - 1], root_recv.at[z - 1], "head", 0
        )

    gives_last = jnp.logical_and(shard == 0, part > 0)

    def root_event(e):
        if 0 < e <= len(seq_steps):
            copy, _, gets = root_over_seq(e - 1)

            @pl.when(gets)
            def _():
                copy.wait_recv()
                root[...] += root_box[head_size - 1 + e - 1]

        if e < len(seq_steps):
            copy, gives, _ = root_over_seq(e)
            pl.when(gives)(copy.start)
        elif e == len(seq_steps):

            @pl.when(gives_last)
            def _():
                root_over_head(jnp.maximum(part, 1)).start()

    root_event(0)
    done = 1
    for k in range(1, head_size):
        to_right, to_left = head_size - k, k - 1
        for c in range(PIECES):

            @pl.when(part == 0)
            def _(d=to_right, c=c):
                going_right(d, c, piece(d, c)).start()

            @pl.when(jnp.logical_and(part > 0, part < to_right))
            def _(d=to_right, c=c):
                going_right(d, c, right_out.at[d, c]).wait_recv()
                right_out[d, c] = (
                    piece(d, c)[...].astype(jnp.float32) + right_in[d, c].astype(jnp.float32)
                ).astype(jnp.bfloat16)
                going_right(d, c, right_out.at[d, c]).start()

            @pl.when(part == head_size - 1)
            def _(d=to_left, c=c):
                going_left(d, c, piece(d, c)).start()

            @pl.when(jnp.logical_and(part < head_size - 1, part > to_left))
            def _(d=to_left, c=c):
                going_left(d, c, left_out.at[d, c]).wait_recv()
                left_out[d, c] = (
                    piece(d, c)[...].astype(jnp.float32) + left_in[d, c].astype(jnp.float32)
                ).astype(jnp.bfloat16)
                going_left(d, c, left_out.at[d, c]).start()

            if c % 2 == 1:
                root_event(done)
                done += 1
    while done <= len(seq_steps):
        root_event(done)
        done += 1
    for c in range(PIECES):
        kv, columns = piece_of(c, width)
        out[:, kv, :, columns] = piece(part, c)[...].astype(jnp.float32)

        @pl.when(part > 0)
        def _(c=c, kv=kv, columns=columns):
            going_right(part, c, right_out.at[part, c]).wait_recv()
            out[:, kv, :, columns] += right_in[part, c].astype(jnp.float32)

        @pl.when(part < head_size - 1)
        def _(c=c, kv=kv, columns=columns):
            going_left(part, c, left_out.at[part, c]).wait_recv()
            out[:, kv, :, columns] += left_in[part, c].astype(jnp.float32)

    @pl.when(jnp.logical_and(shard == 0, part == 0))
    def _():
        for z in range(1, head_size):
            root_over_head(z).wait_recv()
            root[...] += root_box[z - 1]

    root_out[...] = root[...]
    for d in range(head_size):
        for c in range(PIECES):
            pl.when(part < d)(going_right(d, c, right_out.at[d, c]).wait_send)
            pl.when(part > d)(going_left(d, c, left_out.at[d, c]).wait_send)
    for e in range(len(seq_steps)):
        copy, gives, _ = root_over_seq(e)
        pl.when(gives)(copy.wait_send)

    @pl.when(gives_last)
    def _():
        root_over_head(jnp.maximum(part, 1)).wait_send()


def scatter(placed, root, head_size, seq_size):
    count = placed[0].shape[0]
    width = root.shape[-1]
    blocks = count // head_size
    events = head_size - 1 + len(tree_steps(seq_size))
    half = width * 2 // PIECES
    vmem = pltpu.MemorySpace.VMEM
    box = pltpu.VMEM((head_size, PIECES, blocks, BLOCK, half), jnp.bfloat16)
    line = pltpu.SemaphoreType.DMA((head_size, PIECES))
    return pl.pallas_call(
        functools.partial(scatter_kernel, head_size, seq_size),
        in_specs=[pl.BlockSpec(memory_space=vmem)] * (CHUNKS + 1),
        out_specs=[pl.BlockSpec(memory_space=vmem)] * 2,
        out_shape=[
            jax.ShapeDtypeStruct((blocks, 2, BLOCK, width), jnp.float32),
            jax.ShapeDtypeStruct(root.shape, jnp.float32),
        ],
        scratch_shapes=[
            pltpu.VMEM(root.shape, jnp.float32),
            pltpu.VMEM((events,) + root.shape, jnp.float32),
            box, box, box, box,
            line, line, line, line,
            pltpu.SemaphoreType.DMA((events,)),
            pltpu.SemaphoreType.DMA((events,)),
        ],
        compiler_params=pltpu.CompilerParams(
            collective_id=1, has_side_effects=True, vmem_limit_bytes=48 * 1024 * 1024
        ),
        name="scatter",
    )(*placed, root)


def local(queries, key_rows, value_rows, upstream, ancestors):
    tokens, width = key_rows.shape
    blocks = tokens // BLOCK
    shard_blocks = ancestors.shape[0]
    both = ("seq", "head")
    shard, part = lax.axis_index("seq"), lax.axis_index("head")
    origin = shard * shard_blocks
    mine = lax.dynamic_slice_in_dim(ancestors, part * blocks, blocks, 0)
    first_entry, last_entry = mine[:, 0], mine[:, 1]
    use_prev = first_entry >= 0
    use_rand = (last_entry >= 0) & (last_entry != first_entry)
    info = jnp.concatenate(
        [
            (origin + part * blocks)[None].astype(jnp.int32),
            jnp.stack([use_prev, use_rand], 1).reshape(-1).astype(jnp.int32),
        ]
    )
    wanted_near = shifted(last_entry, "seq", -1) - origin
    wanted_far = shifted(last_entry, "seq", -2) - origin
    wanted_own = last_entry - origin
    length = lax.axis_size("seq")
    wanted_near = jnp.where(shard + 1 < length, wanted_near, -1)
    wanted_far = jnp.where(shard + 2 < length, wanted_far, -1)
    wanted = jnp.concatenate([wanted_own, wanted_near, wanted_far]).astype(jnp.int32)

    own = jnp.stack(
        [key_rows.reshape(blocks, BLOCK, width), value_rows.reshape(blocks, BLOCK, width)], 1
    )
    chunk_heads = width // HEAD_SIZE // CHUNKS
    head_size, seq_size = lax.axis_size("head"), length
    is_first = (shard == 0) & (part == 0)
    edge = shifted(own[-1:], both, 1)
    back = (shard - last_entry // shard_blocks).astype(jnp.int32)
    rand, root = gather(wanted, back, own, head_size, seq_size)
    outs = None
    g_owns, g_prevs, placed, g_roots = [], [], [], []
    for c in range(CHUNKS):
        attended, query_grad, g_own, g_prev, g_rand, g_root = attention(
            info, queries, upstream, own, edge, root, rand, outs, c, chunk_heads
        )
        outs = (attended, query_grad)
        near = shifted(g_rand, "seq", -1)
        far = shifted(g_rand, "seq", -2)
        placed.append(place(wanted, g_rand, near, far, shard_blocks))
        g_owns.append(g_own)
        g_prevs.append(g_prev)
        g_roots.append(g_root)
    g_own, g_prev = jnp.concatenate(g_owns, -1), jnp.concatenate(g_prevs, -1)
    g_edge = shifted(g_prev[:1].astype(jnp.bfloat16), both, -1).astype(jnp.float32)
    summed, g_root = scatter(
        placed, jnp.concatenate(g_roots, -1), head_size, seq_size
    )
    total = g_own + summed + jnp.concatenate([g_prev[1:], g_edge], 0)
    head_of_row = jnp.where(is_first, g_root, 0.0)
    total = jnp.concatenate([total[:1] + head_of_row[None], total[1:]], 0)
    total = total.astype(jnp.bfloat16)
    return (
        outs[0],
        outs[1],
        total[:, 0].reshape(tokens, width),
        total[:, 1].reshape(tokens, width),
    )


def solution(mesh):
    tokens = P(("seq", "head"), None)
    return jax.shard_map(
        local,
        mesh=mesh,
        in_specs=(tokens, tokens, tokens, tokens, P("seq", None)),
        out_specs=(tokens, tokens, tokens, tokens),
        check_vma=False,
    )
```
